256 devices in a mesh: rows: 32 (over z, x), cols: 8 (over y, core).
Axes of the slice: x: 4, y: 4, z: 8, core: 2. Of those that a mesh axis runs over, the one named last changes fastest.
Arguments:
- image: bfloat16 [512, 1536, 192], P('rows', 'cols'), may hold values from -6 to 6
- conv_kernel: float32 [7, 7, 192], replicated, may hold values from -0.875 to 0.875
- conv_bias: float32 [192], replicated, may hold values from -3 to 3
- norm_gain: float32 [192], replicated, may hold values from 0.5 to 1.5
- norm_bias: float32 [192], replicated, may hold values from -3 to 3
- in_weight: bfloat16 [192, 768], replicated, may hold values from -0.4375 to 0.4375
- in_bias: float32 [768], replicated, may hold values from -3 to 3
- out_weight: bfloat16 [768, 192], replicated, may hold values from -0.21875 to 0.21875
- out_bias: float32 [192], replicated, may hold values from -3 to 3
- layer_scale: float32 [192], replicated, may hold values from 0.5 to 1.5
- cotangent: bfloat16 [512, 1536, 192], P('rows', 'cols'), may hold values from -6 to 6
Outputs:
- output: bfloat16 [512, 1536, 192], P('rows', 'cols')
- grad_image: bfloat16 [512, 1536, 192], P('rows', 'cols')
- grad_kernel: float32 [7, 7, 192], replicated
- grad_conv_bias: float32 [192], replicated
- grad_gain: float32 [192], replicated
- grad_norm_bias: float32 [192], replicated
- grad_in_weight: float32 [192, 768], P(None, 'rows')
- grad_in_bias: float32 [768], P('rows')
- grad_out_weight: float32 [768, 192], P('rows')
- grad_out_bias: float32 [192], replicated
- grad_scale: float32 [192], replicated
The draws below stay inside these ranges and needn't reach their ends.
All inputs are finite; a program needn't handle non-finite values.
Results may differ from the reference program's by a relative error of at most 0.0062.
Values may be sent and summed in bfloat16 or wider, within the bound.
A program may use at most 192 MiB of HBM per device.

```python
import math
import jax
import jax.numpy as jnp
from jax import lax

C = 192
HID = 768
RD = 16
IMG_H = 512
IMG_W = 1536


def block_scale(key, extent, pieces, least, top_value):
    factor_of = 1.0
    for dim, blocks in pieces:
        draws = jax.random.uniform(jax.random.fold_in(jax.random.fold_in(key, 6), dim), (blocks,), jnp.float32, least / len(pieces), top_value / len(pieces))
        factor_of = factor_of * jnp.repeat(jnp.exp(draws), extent[dim] // blocks).reshape((-1,) + (1,) * (len(extent) - 1 - dim))
    return factor_of


def noise(own_key, dims, width, reach, cuts=(), held_as=jnp.bfloat16):
    loudness = block_scale(own_key, dims, cuts, -0.22, 0.18) if cuts else 1.0
    values = jax.random.normal(own_key, dims, jnp.float32) * width * loudness
    return jnp.minimum(jnp.maximum(values, -reach), reach).astype(held_as)


def setup_inputs(seed: int = 0) -> dict:
    keys = jax.random.split(jax.random.key(seed), 12)
    image = noise(keys[0], (IMG_H, IMG_W, C), 1.0, 6.0, ((0, 32), (1, 8)))
    conv_kernel = noise(keys[1], (7, 7, C), 49 ** -0.5, 0.875, (), jnp.float32)
    conv_bias = noise(keys[2], (C,), 0.5, 3.0, (), jnp.float32)
    norm_gain = jnp.clip(jax.random.uniform(keys[3], (C,), jnp.float32, 0.5, 1.5), 0.5, 1.5)
    norm_bias = noise(keys[4], (C,), 0.5, 3.0, (), jnp.float32)
    in_weight = noise(keys[5], (C, HID), C ** -0.5, 0.4375)
    in_bias = noise(keys[6], (HID,), 0.5, 3.0, (), jnp.float32)
    out_weight = noise(keys[7], (HID, C), HID ** -0.5, 0.21875)
    out_bias = noise(keys[8], (C,), 0.5, 3.0, (), jnp.float32)
    layer_scale = jnp.clip(jax.random.uniform(keys[9], (C,), jnp.float32, 0.5, 1.5), 0.5, 1.5)
    cotangent = noise(keys[10], (IMG_H, IMG_W, C), 1.0, 6.0, ((0, 32), (1, 8)))
    return {"image": image, "conv_kernel": conv_kernel, "conv_bias": conv_bias, "norm_gain": norm_gain, "norm_bias": norm_bias, "in_weight": in_weight, "in_bias": in_bias, "out_weight": out_weight, "out_bias": out_bias, "layer_scale": layer_scale, "cotangent": cotangent}


def gelu_parts(hidden):
    normal_cdf = 0.5 * (1.0 + jax.scipy.special.erf(hidden * 0.7071067811865476))
    normal_pdf = jnp.exp(-0.5 * hidden * hidden) * 0.3989422804014327
    return (hidden * normal_cdf, normal_cdf + hidden * normal_pdf)

def depthwise(padded, conv_kernel, n_rows, n_cols):
    accum = jnp.zeros((n_rows, n_cols, conv_kernel.shape[2]), jnp.float32)
    for row_tap in range(7):
        for col_tap in range(7):
            shifted = padded[row_tap:row_tap + n_rows, col_tap:col_tap + n_cols].astype(jnp.float32)
            accum = accum + shifted * conv_kernel[row_tap, col_tap]
    return accum

def transposed(d_padded, conv_kernel, n_rows, n_cols):
    accum = jnp.zeros((n_rows, n_cols, conv_kernel.shape[2]), jnp.float32)
    for row_tap in range(7):
        for col_tap in range(7):
            shifted = d_padded[6 - row_tap:6 - row_tap + n_rows, 6 - col_tap:6 - col_tap + n_cols].astype(jnp.float32)
            accum = accum + shifted * conv_kernel[row_tap, col_tap]
    return accum

def layer_pass(padded, cotangent, conv_kernel, conv_bias, norm_gain, norm_bias, in_weight, in_bias, out_weight, out_bias, layer_scale):
    n_rows, n_cols, channels = cotangent.shape
    pixels = n_rows * n_cols
    hidden_units = in_weight.shape[1]
    conv_out = depthwise(padded, conv_kernel, n_rows, n_cols) + conv_bias
    average = lax.optimization_barrier(jnp.mean(conv_out, axis=-1, keepdims=True))
    centred = conv_out - average
    inv_std = lax.rsqrt(lax.optimization_barrier(jnp.mean(centred * centred, axis=-1, keepdims=True)) + 1e-06)
    unit_norm = centred * inv_std
    normed = (unit_norm * norm_gain + norm_bias).astype(jnp.bfloat16)
    hidden = jnp.dot(normed.reshape(pixels, channels), in_weight, preferred_element_type=jnp.float32) + in_bias
    act_full, gelu_slope = gelu_parts(hidden)
    activation = act_full.astype(jnp.bfloat16)
    branch = jnp.dot(activation, out_weight, preferred_element_type=jnp.float32) + out_bias
    centre = padded[3:3 + n_rows, 3:3 + n_cols].astype(jnp.float32).reshape(pixels, channels)
    output = (centre + layer_scale * branch).astype(jnp.bfloat16).reshape(n_rows, n_cols, channels)
    cot_full = cotangent.astype(jnp.float32).reshape(pixels, channels)
    scaled = (cot_full * layer_scale).astype(jnp.bfloat16)
    d_act = lax.dot_general(scaled, out_weight, (((1,), (1,)), ((), ())), preferred_element_type=jnp.float32)
    d_hidden_full = d_act * gelu_slope
    d_hidden = d_hidden_full.astype(jnp.bfloat16)
    d_normed = lax.dot_general(d_hidden, in_weight, (((1,), (1,)), ((), ())), preferred_element_type=jnp.float32)
    d_normed = d_normed.reshape(n_rows, n_cols, channels)
    d_unit = d_normed * norm_gain
    d_conv = (d_unit - lax.optimization_barrier(jnp.mean(d_unit, axis=-1, keepdims=True)) - unit_norm * lax.optimization_barrier(jnp.mean(d_unit * unit_norm, axis=-1, keepdims=True))) * inv_std
    shape_c = (n_rows, n_cols, channels)
    shape_h = (n_rows, n_cols, hidden_units)
    return (output, d_conv, unit_norm, normed, activation.reshape(shape_h), scaled.reshape(shape_c), d_hidden.reshape(shape_h), d_hidden_full.reshape(shape_h), d_normed, branch.reshape(shape_c), cot_full.reshape(shape_c))

def partials(results, padded, offset, n_rows, n_cols, layer_scale):
    output, d_conv, unit_norm, normed, activation, scaled, d_hidden, d_hidden_full, d_normed, branch, cot_full = results

    def interior(array):
        return array[offset:offset + n_rows, offset:offset + n_cols].reshape(n_rows * n_cols, array.shape[2])
    d_inner = d_conv[offset:offset + n_rows, offset:offset + n_cols]
    tap_sums = []
    for row_tap in range(7):
        for col_tap in range(7):
            shifted = padded[offset + row_tap:offset + row_tap + n_rows, offset + col_tap:offset + col_tap + n_cols].astype(jnp.float32)
            tap_sums.append(lax.optimization_barrier(jnp.sum(shifted * d_inner, axis=(0, 1))))
    g_kernel = jnp.stack(tap_sums).reshape(7, 7, d_conv.shape[2])
    g_conv_bias = lax.optimization_barrier(jnp.sum(d_inner, axis=(0, 1)))
    g_gain = lax.optimization_barrier(jnp.sum(interior(d_normed) * interior(unit_norm), axis=0))
    g_norm_bias = lax.optimization_barrier(jnp.sum(interior(d_normed), axis=0))
    g_in_weight = lax.dot_general(interior(normed), interior(d_hidden), (((0,), (0,)), ((), ())), preferred_element_type=jnp.float32)
    g_in_bias = lax.optimization_barrier(jnp.sum(interior(d_hidden_full), axis=0))
    g_out_weight = lax.dot_general(interior(activation), interior(scaled), (((0,), (0,)), ((), ())), preferred_element_type=jnp.float32)
    g_out_bias = lax.optimization_barrier(jnp.sum(interior(cot_full), axis=0)) * layer_scale
    g_scale = lax.optimization_barrier(jnp.sum(interior(cot_full) * interior(branch), axis=0))
    return (g_kernel, g_conv_bias, g_gain, g_norm_bias, g_in_weight, g_in_bias, g_out_weight, g_out_bias, g_scale)

def reference(image, conv_kernel, conv_bias, norm_gain, norm_bias, in_weight, in_bias, out_weight, out_bias, layer_scale, cotangent):
    x_padded = jnp.pad(image, ((3, 3), (3, 3), (0, 0)))
    blocks = IMG_H // RD
    zero = jnp.zeros((), jnp.int32)
    starts = jnp.arange(blocks, dtype=jnp.int32) * RD

    def forward_block(totals, row_start):
        padded = lax.dynamic_slice(x_padded, (row_start, zero, zero), (RD + 6, IMG_W + 6, C))
        cot_slab = lax.dynamic_slice(cotangent, (row_start, zero, zero), (RD, IMG_W, C))
        results = layer_pass(padded, cot_slab, conv_kernel, conv_bias, norm_gain, norm_bias, in_weight, in_bias, out_weight, out_bias, layer_scale)
        block_terms = partials(results, padded, 0, RD, IMG_W, layer_scale)
        totals = tuple((a + b for a, b in zip(totals, block_terms)))
        return (totals, (results[0], results[1].astype(jnp.bfloat16)))
    init = (jnp.zeros((7, 7, C), jnp.float32), jnp.zeros((C,), jnp.float32), jnp.zeros((C,), jnp.float32), jnp.zeros((C,), jnp.float32), jnp.zeros((C, HID), jnp.float32), jnp.zeros((HID,), jnp.float32), jnp.zeros((HID, C), jnp.float32), jnp.zeros((C,), jnp.float32), jnp.zeros((C,), jnp.float32))
    totals, (out_blocks, d_blocks) = lax.scan(forward_block, init, starts)
    output = out_blocks.reshape(IMG_H, IMG_W, C)
    d_padded_all = jnp.pad(d_blocks.reshape(IMG_H, IMG_W, C), ((3, 3), (3, 3), (0, 0)))

    def backward_block(row_start):
        d_slab = lax.dynamic_slice(d_padded_all, (row_start, zero, zero), (RD + 6, IMG_W + 6, C))
        cot_slab = lax.dynamic_slice(cotangent, (row_start, zero, zero), (RD, IMG_W, C))
        return (cot_slab.astype(jnp.float32) + transposed(d_slab, conv_kernel, RD, IMG_W)).astype(jnp.bfloat16)
    grad_image = lax.map(backward_block, starts).reshape(IMG_H, IMG_W, C)
    factor = 1.0 / math.sqrt(IMG_H * IMG_W)
    g_kernel, g_conv_bias, g_gain, g_norm_bias, g_in_weight, g_in_bias, g_out_weight, g_out_bias, g_scale = totals
    return (output, grad_image, g_kernel * factor, g_conv_bias * factor, g_gain * factor, g_norm_bias * factor, g_in_weight * factor, g_in_bias * factor, g_out_weight * factor, g_out_bias * factor, g_scale * factor)
```

```python
import functools
import math

import jax
import jax.numpy as jnp
from jax import lax
from jax.experimental import pallas as pl
from jax.experimental.pallas import tpu as pltpu
from jax.sharding import PartitionSpec as P


def padded_2(shard, sides, width):
    for axis, dim in sides:
        peers, length = (lax.axis_size(axis), shard.shape[dim])
        up = [(i, (i + 1) % peers) for i in range(peers - 1)]
        down = [(j, i) for i, j in up]
        last = lax.slice_in_dim(shard, length - width, length, axis=dim)
        first = lax.slice_in_dim(shard, 0, width, axis=dim)
        before = lax.ppermute(last, axis, up)
        after = lax.ppermute(first, axis, down)
        shard = jnp.concatenate([before, shard, after], axis=dim)
    return shard


def gelu_parts(hidden):
    normal_cdf = 0.5 * (1.0 + jax.scipy.special.erf(hidden * 0.7071067811865476))
    normal_pdf = jnp.exp(-0.5 * hidden * hidden) * 0.3989422804014327
    return (hidden * normal_cdf, normal_cdf + hidden * normal_pdf)


def depthwise(padded, conv_kernel, n_rows, n_cols):
    accum = jnp.zeros((n_rows, n_cols, conv_kernel.shape[2]), jnp.float32)
    for row_tap in range(7):
        for col_tap in range(7):
            shifted = padded[row_tap : row_tap + n_rows, col_tap : col_tap + n_cols].astype(
                jnp.float32
            )
            accum = accum + shifted * conv_kernel[row_tap, col_tap]
    return accum


def transposed(d_padded, conv_kernel, n_rows, n_cols):
    accum = jnp.zeros((n_rows, n_cols, conv_kernel.shape[2]), jnp.float32)
    for row_tap in range(7):
        for col_tap in range(7):
            shifted = d_padded[
                6 - row_tap : 6 - row_tap + n_rows, 6 - col_tap : 6 - col_tap + n_cols
            ].astype(jnp.float32)
            accum = accum + shifted * conv_kernel[row_tap, col_tap]
    return accum


def layer_pass(
    padded,
    cotangent,
    conv_kernel,
    conv_bias,
    norm_gain,
    norm_bias,
    in_weight,
    in_bias,
    out_weight,
    out_bias,
    layer_scale,
):
    n_rows, n_cols, channels = cotangent.shape
    pixels = n_rows * n_cols
    hidden_units = in_weight.shape[1]
    conv_out = depthwise(padded, conv_kernel, n_rows, n_cols) + conv_bias
    average = jnp.mean(conv_out, axis=-1, keepdims=True)
    centred = conv_out - average
    inv_std = lax.rsqrt(jnp.mean(centred * centred, axis=-1, keepdims=True) + 1e-06)
    unit_norm = centred * inv_std
    normed = (unit_norm * norm_gain + norm_bias).astype(jnp.bfloat16)
    hidden = (
        jnp.dot(normed.reshape(pixels, channels), in_weight, preferred_element_type=jnp.float32)
        + in_bias
    )
    act_full, gelu_slope = gelu_parts(hidden)
    activation = act_full.astype(jnp.bfloat16)
    branch = jnp.dot(activation, out_weight, preferred_element_type=jnp.float32) + out_bias
    centre = padded[3 : 3 + n_rows, 3 : 3 + n_cols].astype(jnp.float32).reshape(pixels, channels)
    output = (centre + layer_scale * branch).astype(jnp.bfloat16).reshape(n_rows, n_cols, channels)
    cot_full = cotangent.astype(jnp.float32).reshape(pixels, channels)
    scaled = (cot_full * layer_scale).astype(jnp.bfloat16)
    d_act = lax.dot_general(
        scaled, out_weight, (((1,), (1,)), ((), ())), preferred_element_type=jnp.float32
    )
    d_hidden_full = d_act * gelu_slope
    d_hidden = d_hidden_full.astype(jnp.bfloat16)
    d_normed = lax.dot_general(
        d_hidden, in_weight, (((1,), (1,)), ((), ())), preferred_element_type=jnp.float32
    )
    d_normed = d_normed.reshape(n_rows, n_cols, channels)
    d_unit = d_normed * norm_gain
    d_conv = (
        d_unit
        - jnp.mean(d_unit, axis=-1, keepdims=True)
        - unit_norm * jnp.mean(d_unit * unit_norm, axis=-1, keepdims=True)
    ) * inv_std
    shape_c = (n_rows, n_cols, channels)
    shape_h = (n_rows, n_cols, hidden_units)
    return (
        output,
        d_conv,
        unit_norm,
        normed,
        activation.reshape(shape_h),
        scaled.reshape(shape_c),
        d_hidden.reshape(shape_h),
        d_hidden_full.reshape(shape_h),
        d_normed,
        branch.reshape(shape_c),
        cot_full.reshape(shape_c),
    )


def partials(results, padded, offset, n_rows, n_cols, layer_scale):
    (
        output,
        d_conv,
        unit_norm,
        normed,
        activation,
        scaled,
        d_hidden,
        d_hidden_full,
        d_normed,
        branch,
        cot_full,
    ) = results

    def interior(array):
        return array.reshape(n_rows * n_cols, array.shape[2])

    tap_sums = []
    for row_tap in range(7):
        for col_tap in range(7):
            shifted = padded[
                offset + row_tap : offset + row_tap + n_rows,
                offset + col_tap : offset + col_tap + n_cols,
            ].astype(jnp.float32)
            tap_sums.append(jnp.sum(shifted * d_conv, axis=(0, 1)))
    g_kernel = jnp.stack(tap_sums).reshape(7, 7, d_conv.shape[2])
    g_conv_bias = jnp.sum(d_conv, axis=(0, 1))
    g_gain = jnp.sum(interior(d_normed) * interior(unit_norm), axis=0)
    g_norm_bias = jnp.sum(interior(d_normed), axis=0)
    g_in_weight = lax.dot_general(
        interior(normed),
        interior(d_hidden),
        (((0,), (0,)), ((), ())),
        preferred_element_type=jnp.float32,
    )
    g_in_bias = jnp.sum(interior(d_hidden_full), axis=0)
    g_out_weight = lax.dot_general(
        interior(activation),
        interior(scaled),
        (((0,), (0,)), ((), ())),
        preferred_element_type=jnp.float32,
    )
    g_out_bias = jnp.sum(interior(cot_full), axis=0) * layer_scale
    g_scale = jnp.sum(interior(cot_full) * interior(branch), axis=0)
    return (
        g_kernel,
        g_conv_bias,
        g_gain,
        g_norm_bias,
        g_in_weight,
        g_in_bias,
        g_out_weight,
        g_out_bias,
        g_scale,
    )


MESH = pl.DeviceIdType.MESH
SHARE = 24


def reduce_kernel(
    factor,
    w_ref,
    s_ref,
    wout_ref,
    sout_ref,
    core_tx,
    core_rx,
    score_rx,
    row_tx,
    srow_tx,
    row_rx,
    srow_rx,
    col_rx,
    scol_rx,
    gat_tx,
    gat_rx,
    core_send,
    core_recv,
    row_send,
    row_recv,
    col_send,
    col_recv,
    gat_send,
    gat_recv,
):
    row = lax.axis_index("rows")
    col = lax.axis_index("cols")
    core = lax.rem(col, 2)
    pair = col - core
    other = pair + 1 - core
    half = row // 16
    place = lax.rem(row, 16)
    owner = half == core

    barrier = pltpu.get_barrier_semaphore()

    def greet_row(step, carry):
        peer = lax.rem(row + step, 32)
        pl.semaphore_signal(barrier, inc=1, device_id=(peer, col), device_id_type=MESH)
        return carry

    def greet_col(step, carry):
        peer = lax.rem(col + step, 8)
        pl.semaphore_signal(barrier, inc=1, device_id=(row, peer), device_id_type=MESH)
        return carry

    lax.fori_loop(1, 32, greet_row, 0)
    lax.fori_loop(1, 8, greet_col, 0)

    def share_of(index):
        rows = w_ref[pl.ds(pl.multiple_of(index * SHARE, 8), SHARE), :]
        return jnp.concatenate([rows[:, 0:128], rows[:, 128:256], rows[:, 256:384]], axis=0)

    def pack_core(j, carry):
        core_tx[j] = share_of(16 * (1 - core) + j).astype(jnp.bfloat16)
        return carry

    lax.fori_loop(0, 16, pack_core, 0)
    pl.semaphore_wait(barrier, 38)

    to_core = pltpu.make_async_remote_copy(
        core_tx, core_rx, core_send.at[0], core_recv.at[0], device_id=(row, other), device_id_type=MESH
    )
    to_core_s = pltpu.make_async_remote_copy(
        s_ref, score_rx, core_send.at[1], core_recv.at[1], device_id=(row, other), device_id_type=MESH
    )
    to_core.start()
    to_core_s.start()
    to_core.wait()
    to_core_s.wait()

    for j in range(16):
        top, left = 8 * (j // 2), 128 * (j % 2)
        srow_tx[j] = (
            s_ref[top : top + 8, left : left + 128] + score_rx[top : top + 8, left : left + 128]
        )

    def row_copies(j):
        return (
            pltpu.make_async_remote_copy(
                row_tx.at[j],
                row_rx.at[row],
                row_send.at[0, j],
                row_recv.at[0, row],
                device_id=(16 * core + j, col),
                device_id_type=MESH,
            ),
            pltpu.make_async_remote_copy(
                srow_tx.at[j],
                srow_rx.at[row],
                row_send.at[1, j],
                row_recv.at[1, row],
                device_id=(16 * core + j, col),
                device_id_type=MESH,
            ),
        )

    def pack_row(step, carry):
        j = lax.rem(place + step, 16)
        row_tx[j] = (share_of(16 * core + j) + core_rx[j].astype(jnp.float32)).astype(jnp.bfloat16)
        return carry

    def send_row(step, carry):
        j = lax.rem(place + step, 16)

        @pl.when(16 * core + j != row)
        def _():
            for copy in row_copies(j):
                copy.start()

        return carry

    lax.fori_loop(0, 16, pack_row, 0)
    lax.fori_loop(0, 16, send_row, 0)

    def col_copies(step):
        peer = lax.rem(col + step, 8)
        return (
            pltpu.make_async_remote_copy(
                col_rx.at[col // 2],
                col_rx.at[col // 2],
                col_send.at[0, step],
                col_recv.at[0, col // 2],
                device_id=(row, peer),
                device_id_type=MESH,
            ),
            pltpu.make_async_remote_copy(
                scol_rx.at[col // 2],
                scol_rx.at[col // 2],
                col_send.at[1, step],
                col_recv.at[1, col // 2],
                device_id=(row, peer),
                device_id_type=MESH,
            ),
        )

    @pl.when(owner)
    def _():
        row_rx[row] = row_tx[place]
        srow_rx[row] = srow_tx[place]

        def wait_row(step, carry):
            peer = lax.rem(row + step, 32)
            pltpu.make_async_copy(row_tx.at[0], row_rx.at[peer], row_recv.at[0, peer]).wait()
            pltpu.make_async_copy(srow_tx.at[0], srow_rx.at[peer], row_recv.at[1, peer]).wait()
            return carry

        lax.fori_loop(1, 32, wait_row, 0)

        def add_row(i, carry):
            return (carry[0] + row_rx[i].astype(jnp.float32), carry[1] + srow_rx[i])

        total, s_total = lax.fori_loop(
            0, 32, add_row, (jnp.zeros((72, 128), jnp.float32), jnp.zeros((8, 128), jnp.float32))
        )
        col_rx[col // 2] = total.astype(jnp.bfloat16)
        scol_rx[col // 2] = s_total

        def send_col(step, carry):
            for copy in col_copies(step):
                copy.start()
            return carry

        lax.fori_loop(1, 8, send_col, 0)

    def wait_col(y, carry):
        @pl.when(2 * y + half != col)
        def _():
            pltpu.make_async_copy(col_rx.at[y], col_rx.at[y], col_recv.at[0, y]).wait()
            pltpu.make_async_copy(scol_rx.at[y], scol_rx.at[y], col_recv.at[1, y]).wait()

        return carry

    lax.fori_loop(0, 4, wait_col, 0)
    block = (scol_rx[0] + scol_rx[1]) + (scol_rx[2] + scol_rx[3])
    gat_tx[...] = block * factor
    share = jnp.zeros((72, 128), jnp.float32)
    for y in range(4):
        share = share + col_rx[y].astype(jnp.float32)
    share = share * factor

    def gather_copy(step):
        peer = 16 * half + lax.rem(place + step, 16)
        return pltpu.make_async_remote_copy(
            gat_tx,
            gat_rx.at[place],
            gat_send.at[step],
            gat_recv.at[place],
            device_id=(peer, col),
            device_id_type=MESH,
        )

    def send_gather(step, carry):
        gather_copy(step).start()
        return carry

    lax.fori_loop(1, 16, send_gather, 0)
    for k in range(3):
        wout_ref[:, 128 * k : 128 * (k + 1)] = share[SHARE * k : SHARE * (k + 1)]
    gat_rx[place] = gat_tx[...]

    def wait_gather(step, carry):
        peer = lax.rem(place + step, 16)
        pltpu.make_async_copy(gat_tx, gat_rx.at[peer], gat_recv.at[peer]).wait()
        return carry

    lax.fori_loop(1, 16, wait_gather, 0)
    for j in range(16):
        top, left = 8 * (j // 2), 128 * (j % 2)
        sout_ref[top : top + 8, left : left + 128] = gat_rx[j]

    def drain_row(step, carry):
        j = lax.rem(place + step, 16)

        @pl.when(16 * core + j != row)
        def _():
            for copy in row_copies(j):
                copy.wait_send()

        return carry

    lax.fori_loop(0, 16, drain_row, 0)

    @pl.when(owner)
    def _():
        def drain_col(step, carry):
            for copy in col_copies(step):
                copy.wait_send()
            return carry

        lax.fori_loop(1, 8, drain_col, 0)

    def drain_gather(step, carry):
        gather_copy(step).wait_send()
        return carry

    lax.fori_loop(1, 16, drain_gather, 0)


def reduce_all(w_sum, s_sum, factor):
    vmem = pl.BlockSpec(memory_space=pltpu.VMEM)
    dma = pltpu.SemaphoreType.DMA
    return pl.pallas_call(
        functools.partial(reduce_kernel, factor),
        out_shape=(
            jax.ShapeDtypeStruct((SHARE, 384), jnp.float32),
            jax.ShapeDtypeStruct((64, 256), jnp.float32),
        ),
        in_specs=[vmem, vmem],
        out_specs=(vmem, vmem),
        scratch_shapes=[
            pltpu.VMEM((16, 72, 128), jnp.bfloat16),
            pltpu.VMEM((16, 72, 128), jnp.bfloat16),
            pltpu.VMEM((64, 256), jnp.float32),
            pltpu.VMEM((16, 72, 128), jnp.bfloat16),
            pltpu.VMEM((16, 8, 128), jnp.float32),
            pltpu.VMEM((32, 72, 128), jnp.bfloat16),
            pltpu.VMEM((32, 8, 128), jnp.float32),
            pltpu.VMEM((4, 72, 128), jnp.bfloat16),
            pltpu.VMEM((4, 8, 128), jnp.float32),
            pltpu.VMEM((8, 128), jnp.float32),
            pltpu.VMEM((16, 8, 128), jnp.float32),
            dma((2,)),
            dma((2,)),
            dma((2, 16)),
            dma((2, 32)),
            dma((2, 8)),
            dma((2, 4)),
            dma((16,)),
            dma((16,)),
        ],
        compiler_params=pltpu.CompilerParams(collective_id=0, has_side_effects=True),
    )(w_sum, s_sum)


def body(
    image,
    conv_kernel,
    conv_bias,
    norm_gain,
    norm_bias,
    in_weight,
    in_bias,
    out_weight,
    out_bias,
    layer_scale,
    cotangent,
):
    n_rows, n_cols, channels = image.shape
    padded = padded_2(image, (("rows", 0), ("cols", 1)), 3)
    results = layer_pass(
        padded,
        cotangent,
        conv_kernel,
        conv_bias,
        norm_gain,
        norm_bias,
        in_weight,
        in_bias,
        out_weight,
        out_bias,
        layer_scale,
    )
    output = results[0]
    d_padded = padded_2(results[1].astype(jnp.bfloat16), (("rows", 0), ("cols", 1)), 3)
    grad_terms = partials(results, padded, 0, n_rows, n_cols, layer_scale)
    grad_image = (
        cotangent.astype(jnp.float32) + transposed(d_padded, conv_kernel, n_rows, n_cols)
    ).astype(jnp.bfloat16)
    (
        g_kernel,
        g_conv_bias,
        g_gain,
        g_norm_bias,
        g_in_weight,
        g_in_bias,
        g_out_weight,
        g_out_bias,
        g_scale,
    ) = grad_terms
    factor = 1.0 / math.sqrt(n_rows * lax.axis_size("rows") * n_cols * lax.axis_size("cols"))
    hidden_units = in_weight.shape[1]
    w_sum = jnp.concatenate([g_in_weight.T, g_out_weight], axis=1)
    s_sum = jnp.concatenate(
        [
            g_kernel.reshape(49, channels),
            g_conv_bias[None],
            g_gain[None],
            g_norm_bias[None],
            g_out_bias[None],
            g_scale[None],
            g_in_bias.reshape(4, channels),
        ],
        axis=0,
    )
    s_sum = jnp.pad(s_sum, ((0, 6), (0, 64)))
    w_share, s_all = reduce_all(w_sum, s_sum, factor)
    s_all = s_all[:, :channels]
    bias_all = s_all[54:58].reshape(hidden_units)
    bias_share = lax.dynamic_slice(bias_all, (lax.axis_index("rows") * SHARE,), (SHARE,))
    return (
        output,
        grad_image,
        s_all[:49].reshape(7, 7, channels),
        s_all[49],
        s_all[50],
        s_all[51],
        w_share[:, :channels].T,
        bias_share,
        w_share[:, channels:],
        s_all[52],
        s_all[53],
    )


def solution(mesh):
    placed = (
        P("rows", "cols", None),
        P(),
        P(),
        P(),
        P(),
        P(),
        P(),
        P(),
        P(),
        P(),
        P("rows", "cols", None),
    )
    return jax.shard_map(
        body,
        mesh=mesh,
        in_specs=placed,
        out_specs=(
            P("rows", "cols", None),
            P("rows", "cols", None),
            P(),
            P(),
            P(),
            P(),
            P(None, "rows"),
            P("rows"),
            P("rows", None),
            P(),
            P(),
        ),
        check_vma=False,
    )
```

```python
import functools
import math

import jax
import jax.numpy as jnp
from jax import lax
from jax.experimental import pallas as pl
from jax.experimental.pallas import tpu as pltpu
from jax.sharding import PartitionSpec as P


def padded_2(shard, sides, width):
    for axis, dim in sides:
        peers, length = (lax.axis_size(axis), shard.shape[dim])
        up = [(i, (i + 1) % peers) for i in range(peers - 1)]
        down = [(j, i) for i, j in up]
        last = lax.slice_in_dim(shard, length - width, length, axis=dim)
        first = lax.slice_in_dim(shard, 0, width, axis=dim)
        before = lax.ppermute(last, axis, up)
        after = lax.ppermute(first, axis, down)
        shard = jnp.concatenate([before, shard, after], axis=dim)
    return shard


def gelu_parts(hidden):
    normal_cdf = 0.5 * (1.0 + jax.scipy.special.erf(hidden * 0.7071067811865476))
    normal_pdf = jnp.exp(-0.5 * hidden * hidden) * 0.3989422804014327
    return (hidden * normal_cdf, normal_cdf + hidden * normal_pdf)


def widen(source_ref, main_ref, rest_ref):
    n_rows, n_cols, _ = source_ref.shape

    def step(i, carry):
        row = source_ref[i].astype(jnp.float32)
        row = jnp.concatenate([row, jnp.zeros((200 - n_cols, 192), jnp.float32)], axis=0)
        main_ref[i] = row[:, 0:128]
        rest_ref[i] = jnp.concatenate([row[0:104, 128:192], row[96:200, 128:192]], axis=1)
        return carry

    lax.fori_loop(0, n_rows, step, 0)


def tile_of(wide_ref, taps_ref, first, start, flip):
    n_rows = wide_ref.shape[0] - 6
    accum = jnp.zeros((n_rows, 8, 128), jnp.float32)
    for b in range(7):
        shifted = wide_ref[:, pl.ds(start + b, 8), :]
        for a in range(7):
            tap = 48 - (7 * a + b) if flip else 7 * a + b
            accum = accum + shifted[a : a + n_rows] * taps_ref[tap, first : first + 128]
    return accum


def convolve(main_ref, rest_ref, taps_ref, flip, out_ref):
    def main_step(i, carry):
        start = pl.multiple_of(8 * i, 8)
        out_ref[:, pl.ds(start, 8), 0:128] = tile_of(main_ref, taps_ref, 0, start, flip)
        return carry

    def rest_step(i, carry):
        start = pl.multiple_of(8 * i, 8)
        tile = tile_of(rest_ref, taps_ref, 128, start, flip)
        out_ref[:, pl.ds(start, 8), 128:192] = tile[:, :, 0:64]
        out_ref[:, pl.ds(start + 96, 8), 128:192] = tile[:, :, 64:128]
        return carry

    lax.fori_loop(0, 24, main_step, 0)
    lax.fori_loop(0, 12, rest_step, 0)


def tap_sums(main_ref, rest_ref, d_main_ref, d_rest_ref, sums_ref):
    n_rows = d_main_ref.shape[0]
    for wide_ref, d_ref, first, steps in (
        (main_ref, d_main_ref, 0, 24),
        (rest_ref, d_rest_ref, 128, 12),
    ):

        def step(i, carry, wide_ref=wide_ref, d_ref=d_ref, first=first):
            start = pl.multiple_of(8 * i, 8)
            d_tile = d_ref[:, pl.ds(start, 8), :]
            for b in range(7):
                shifted = wide_ref[:, pl.ds(start + b, 8), :]
                for a in range(7):
                    tap = 7 * a + b
                    sums_ref[tap, :, first : first + 128] += jnp.sum(
                        shifted[a : a + n_rows] * d_tile, axis=0
                    )
            return carry

        lax.fori_loop(0, steps, step, 0)


def fold(values):
    return jnp.sum(values.reshape(values.shape[0] // 8, 8, values.shape[1]), axis=0)


CHUNK = 2


def block_kernel(
    padded_ref,
    image_ref,
    cot_ref,
    taps_ref,
    rows_ref,
    in_weight_ref,
    in_weight_t_ref,
    in_bias_ref,
    out_weight_ref,
    out_weight_t_ref,
    output_ref,
    d_conv_ref,
    w_ref,
    s_ref,
    main_ref,
    rest_ref,
    conv_ref,
    d_main_ref,
    d_rest_ref,
    sums_ref,
    tap_ref,
    bias_sum_ref,
    g_in_ref,
    g_out_ref,
):
    n_rows, n_cols, channels = image_ref.shape
    pixels = CHUNK * n_cols
    widen(padded_ref, main_ref, rest_ref)
    sums_ref[...] = jnp.zeros_like(sums_ref)
    tap_ref[...] = jnp.zeros_like(tap_ref)
    bias_sum_ref[...] = jnp.zeros_like(bias_sum_ref)
    g_in_ref[...] = jnp.zeros_like(g_in_ref)
    g_out_ref[...] = jnp.zeros_like(g_out_ref)

    convolve(main_ref, rest_ref, taps_ref, False, conv_ref)

    def chunk(i, carry):
        span = pl.ds(CHUNK * i, CHUNK)
        conv_bias, gain, norm_bias = rows_ref[0:1], rows_ref[1:2], rows_ref[2:3]
        out_bias, layer_scale = rows_ref[3:4], rows_ref[4:5]
        conv_out = conv_ref[span].reshape(pixels, channels) + conv_bias
        centred = conv_out - jnp.mean(conv_out, axis=-1, keepdims=True)
        inv_std = lax.rsqrt(jnp.mean(centred * centred, axis=-1, keepdims=True) + 1e-06)
        unit_norm = centred * inv_std
        normed = (unit_norm * gain + norm_bias).astype(jnp.bfloat16)
        hidden = (
            jnp.dot(normed, in_weight_ref[...], preferred_element_type=jnp.float32) + in_bias_ref[...]
        )
        act_full, gelu_slope = gelu_parts(hidden)
        activation = act_full.astype(jnp.bfloat16)
        branch = (
            jnp.dot(activation, out_weight_ref[...], preferred_element_type=jnp.float32) + out_bias
        )
        centre = image_ref[span].astype(jnp.float32).reshape(pixels, channels)
        output_ref[span] = (
            (centre + layer_scale * branch).astype(jnp.bfloat16).reshape(CHUNK, n_cols, channels)
        )
        cot_full = cot_ref[span].astype(jnp.float32).reshape(pixels, channels)
        scaled = (cot_full * layer_scale).astype(jnp.bfloat16)
        d_act = jnp.dot(scaled, out_weight_t_ref[...], preferred_element_type=jnp.float32)
        d_hidden_full = d_act * gelu_slope
        d_hidden = d_hidden_full.astype(jnp.bfloat16)
        d_normed = jnp.dot(d_hidden, in_weight_t_ref[...], preferred_element_type=jnp.float32)
        d_unit = d_normed * gain
        d_conv = (
            d_unit
            - jnp.mean(d_unit, axis=-1, keepdims=True)
            - unit_norm * jnp.mean(d_unit * unit_norm, axis=-1, keepdims=True)
        ) * inv_std
        d_conv_3 = d_conv.reshape(CHUNK, n_cols, channels)
        d_main_ref[span] = d_conv_3[:, :, 0:128]
        d_rest_ref[span] = jnp.concatenate(
            [d_conv_3[:, 0:96, 128:192], d_conv_3[:, 96:192, 128:192]], axis=2
        )
        d_conv_ref[span] = d_conv_3.astype(jnp.bfloat16)
        contract = (((0,), (0,)), ((), ()))
        g_in_ref[...] += lax.dot_general(
            normed, d_hidden, contract, preferred_element_type=jnp.float32
        )
        g_out_ref[...] += lax.dot_general(
            scaled, activation, contract, preferred_element_type=jnp.float32
        )
        bias_sum_ref[...] += fold(d_hidden_full)
        sums_ref[0] += fold(d_conv)
        sums_ref[1] += fold(d_normed * unit_norm)
        sums_ref[2] += fold(d_normed)
        sums_ref[3] += fold(cot_full)
        sums_ref[4] += fold(cot_full * branch)
        return carry

    lax.fori_loop(0, n_rows // CHUNK, chunk, 0)
    tap_sums(main_ref, rest_ref, d_main_ref, d_rest_ref, tap_ref)

    s_ref[...] = jnp.zeros_like(s_ref)
    taps = jnp.sum(tap_ref[...], axis=1)
    s_ref[0:49, 0:128] = taps[:, 0:128]
    s_ref[0:49, 128:192] = taps[:, 128:192] + taps[:, 192:256]
    s_ref[49:54, 0:channels] = jnp.sum(sums_ref[...], axis=1)
    s_ref[52:53, 0:channels] = s_ref[52:53, 0:channels] * rows_ref[4:5]
    bias_sum = jnp.sum(bias_sum_ref[...], axis=0, keepdims=True)
    for k in range(4):
        s_ref[54 + k : 55 + k, 0:channels] = bias_sum[:, channels * k : channels * (k + 1)]
    w_ref[:, 0:channels] = g_in_ref[...].T
    w_ref[:, channels : 2 * channels] = g_out_ref[...].T


VMEM_LIMIT = 64 * 1024 * 1024 - 65536


def block(padded, image, cotangent, taps, rows, in_weight, in_bias, out_weight):
    n_rows, n_cols, channels = image.shape
    hidden_units = in_weight.shape[1]
    vmem = pl.BlockSpec(memory_space=pltpu.VMEM)
    f32 = jnp.float32
    return pl.pallas_call(
        block_kernel,
        out_shape=(
            jax.ShapeDtypeStruct(image.shape, jnp.bfloat16),
            jax.ShapeDtypeStruct(image.shape, jnp.bfloat16),
            jax.ShapeDtypeStruct((hidden_units, 2 * channels), f32),
            jax.ShapeDtypeStruct((64, 256), f32),
        ),
        in_specs=[vmem] * 10,
        out_specs=(vmem,) * 4,
        scratch_shapes=[
            pltpu.VMEM((n_rows + 6, 200, 128), f32),
            pltpu.VMEM((n_rows + 6, 104, 128), f32),
            pltpu.VMEM((n_rows, n_cols, channels), f32),
            pltpu.VMEM((n_rows, n_cols, 128), f32),
            pltpu.VMEM((n_rows, n_cols // 2, 128), f32),
            pltpu.VMEM((5, 8, channels), f32),
            pltpu.VMEM((49, 8, 256), f32),
            pltpu.VMEM((8, hidden_units), f32),
            pltpu.VMEM((channels, hidden_units), f32),
            pltpu.VMEM((channels, hidden_units), f32),
        ],
        compiler_params=pltpu.CompilerParams(vmem_limit_bytes=VMEM_LIMIT),
    )(
        padded,
        image,
        cotangent,
        taps,
        rows,
        in_weight,
        in_weight.T,
        in_bias[None],
        out_weight,
        out_weight.T,
    )


def transposed_kernel(padded_ref, cot_ref, taps_ref, out_ref, main_ref, rest_ref, conv_ref):
    widen(padded_ref, main_ref, rest_ref)

    convolve(main_ref, rest_ref, taps_ref, True, conv_ref)

    def step(i, carry):
        out_ref[i] = (cot_ref[i].astype(jnp.float32) + conv_ref[i]).astype(jnp.bfloat16)
        return carry

    lax.fori_loop(0, cot_ref.shape[0], step, 0)


def transposed_conv(d_padded, cotangent, taps):
    n_rows, n_cols, channels = cotangent.shape
    vmem = pl.BlockSpec(memory_space=pltpu.VMEM)
    return pl.pallas_call(
        transposed_kernel,
        out_shape=jax.ShapeDtypeStruct(cotangent.shape, jnp.bfloat16),
        in_specs=[vmem] * 3,
        out_specs=vmem,
        scratch_shapes=[
            pltpu.VMEM((n_rows + 6, 200, 128), jnp.float32),
            pltpu.VMEM((n_rows + 6, 104, 128), jnp.float32),
            pltpu.VMEM((n_rows, n_cols, channels), jnp.float32),
        ],
        compiler_params=pltpu.CompilerParams(vmem_limit_bytes=VMEM_LIMIT),
    )(d_padded, cotangent, taps)


MESH = pl.DeviceIdType.MESH
SHARE = 24


def reduce_kernel(
    factor,
    w_ref,
    s_ref,
    wout_ref,
    sout_ref,
    core_tx,
    core_rx,
    score_rx,
    row_tx,
    srow_tx,
    row_rx,
    srow_rx,
    col_rx,
    scol_rx,
    gat_tx,
    gat_rx,
    core_send,
    core_recv,
    row_send,
    row_recv,
    col_send,
    col_recv,
    gat_send,
    gat_recv,
):
    row = lax.axis_index("rows")
    col = lax.axis_index("cols")
    core = lax.rem(col, 2)
    pair = col - core
    other = pair + 1 - core
    half = row // 16
    place = lax.rem(row, 16)
    owner = half == core

    barrier = pltpu.get_barrier_semaphore()

    def greet_row(step, carry):
        peer = lax.rem(row + step, 32)
        pl.semaphore_signal(barrier, inc=1, device_id=(peer, col), device_id_type=MESH)
        return carry

    def greet_col(step, carry):
        peer = lax.rem(col + step, 8)
        pl.semaphore_signal(barrier, inc=1, device_id=(row, peer), device_id_type=MESH)
        return carry

    lax.fori_loop(1, 32, greet_row, 0)
    lax.fori_loop(1, 8, greet_col, 0)

    def share_of(index):
        rows = w_ref[pl.ds(pl.multiple_of(index * SHARE, 8), SHARE), :]
        return jnp.concatenate([rows[:, 0:128], rows[:, 128:256], rows[:, 256:384]], axis=0)

    def pack_core(j, carry):
        core_tx[j] = share_of(16 * (1 - core) + j).astype(jnp.bfloat16)
        return carry

    lax.fori_loop(0, 16, pack_core, 0)
    pl.semaphore_wait(barrier, 38)

    to_core = pltpu.make_async_remote_copy(
        core_tx, core_rx, core_send.at[0], core_recv.at[0], device_id=(row, other), device_id_type=MESH
    )
    to_core_s = pltpu.make_async_remote_copy(
        s_ref, score_rx, core_send.at[1], core_recv.at[1], device_id=(row, other), device_id_type=MESH
    )
    to_core.start()
    to_core_s.start()
    to_core.wait()
    to_core_s.wait()

    for j in range(16):
        top, left = 8 * (j // 2), 128 * (j % 2)
        srow_tx[j] = (
            s_ref[top : top + 8, left : left + 128] + score_rx[top : top + 8, left : left + 128]
        )

    def row_copies(j):
        return (
            pltpu.make_async_remote_copy(
                row_tx.at[j],
                row_rx.at[row],
                row_send.at[0, j],
                row_recv.at[0, row],
                device_id=(16 * core + j, col),
                device_id_type=MESH,
            ),
            pltpu.make_async_remote_copy(
                srow_tx.at[j],
                srow_rx.at[row],
                row_send.at[1, j],
                row_recv.at[1, row],
                device_id=(16 * core + j, col),
                device_id_type=MESH,
            ),
        )

    def pack_row(step, carry):
        j = lax.rem(place + step, 16)
        row_tx[j] = (share_of(16 * core + j) + core_rx[j].astype(jnp.float32)).astype(jnp.bfloat16)
        return carry

    def send_row(step, carry):
        j = lax.rem(place + step, 16)

        @pl.when(16 * core + j != row)
        def _():
            for copy in row_copies(j):
                copy.start()

        return carry

    lax.fori_loop(0, 16, pack_row, 0)
    lax.fori_loop(0, 16, send_row, 0)

    def col_copies(step):
        peer = lax.rem(col + step, 8)
        return (
            pltpu.make_async_remote_copy(
                col_rx.at[col // 2],
                col_rx.at[col // 2],
                col_send.at[0, step],
                col_recv.at[0, col // 2],
                device_id=(row, peer),
                device_id_type=MESH,
            ),
            pltpu.make_async_remote_copy(
                scol_rx.at[col // 2],
                scol_rx.at[col // 2],
                col_send.at[1, step],
                col_recv.at[1, col // 2],
                device_id=(row, peer),
                device_id_type=MESH,
            ),
        )

    @pl.when(owner)
    def _():
        row_rx[row] = row_tx[place]
        srow_rx[row] = srow_tx[place]

        def wait_row(step, carry):
            peer = lax.rem(row + step, 32)
            pltpu.make_async_copy(row_tx.at[0], row_rx.at[peer], row_recv.at[0, peer]).wait()
            pltpu.make_async_copy(srow_tx.at[0], srow_rx.at[peer], row_recv.at[1, peer]).wait()
            return carry

        lax.fori_loop(1, 32, wait_row, 0)

        def add_row(i, carry):
            return (carry[0] + row_rx[i].astype(jnp.float32), carry[1] + srow_rx[i])

        total, s_total = lax.fori_loop(
            0, 32, add_row, (jnp.zeros((72, 128), jnp.float32), jnp.zeros((8, 128), jnp.float32))
        )
        col_rx[col // 2] = total.astype(jnp.bfloat16)
        scol_rx[col // 2] = s_total

        def send_col(step, carry):
            for copy in col_copies(step):
                copy.start()
            return carry

        lax.fori_loop(1, 8, send_col, 0)

    def wait_col(y, carry):
        @pl.when(2 * y + half != col)
        def _():
            pltpu.make_async_copy(col_rx.at[y], col_rx.at[y], col_recv.at[0, y]).wait()
            pltpu.make_async_copy(scol_rx.at[y], scol_rx.at[y], col_recv.at[1, y]).wait()

        return carry

    lax.fori_loop(0, 4, wait_col, 0)
    block = (scol_rx[0] + scol_rx[1]) + (scol_rx[2] + scol_rx[3])
    gat_tx[...] = block * factor
    share = jnp.zeros((72, 128), jnp.float32)
    for y in range(4):
        share = share + col_rx[y].astype(jnp.float32)
    share = share * factor

    def gather_copy(step):
        peer = 16 * half + lax.rem(place + step, 16)
        return pltpu.make_async_remote_copy(
            gat_tx,
            gat_rx.at[place],
            gat_send.at[step],
            gat_recv.at[place],
            device_id=(peer, col),
            device_id_type=MESH,
        )

    def send_gather(step, carry):
        gather_copy(step).start()
        return carry

    lax.fori_loop(1, 16, send_gather, 0)
    for k in range(3):
        wout_ref[:, 128 * k : 128 * (k + 1)] = share[SHARE * k : SHARE * (k + 1)]
    gat_rx[place] = gat_tx[...]

    def wait_gather(step, carry):
        peer = lax.rem(place + step, 16)
        pltpu.make_async_copy(gat_tx, gat_rx.at[peer], gat_recv.at[peer]).wait()
        return carry

    lax.fori_loop(1, 16, wait_gather, 0)
    for j in range(16):
        top, left = 8 * (j // 2), 128 * (j % 2)
        sout_ref[top : top + 8, left : left + 128] = gat_rx[j]

    def drain_row(step, carry):
        j = lax.rem(place + step, 16)

        @pl.when(16 * core + j != row)
        def _():
            for copy in row_copies(j):
                copy.wait_send()

        return carry

    lax.fori_loop(0, 16, drain_row, 0)

    @pl.when(owner)
    def _():
        def drain_col(step, carry):
            for copy in col_copies(step):
                copy.wait_send()
            return carry

        lax.fori_loop(1, 8, drain_col, 0)

    def drain_gather(step, carry):
        gather_copy(step).wait_send()
        return carry

    lax.fori_loop(1, 16, drain_gather, 0)


def reduce_all(w_sum, s_sum, factor):
    vmem = pl.BlockSpec(memory_space=pltpu.VMEM)
    dma = pltpu.SemaphoreType.DMA
    return pl.pallas_call(
        functools.partial(reduce_kernel, factor),
        out_shape=(
            jax.ShapeDtypeStruct((SHARE, 384), jnp.float32),
            jax.ShapeDtypeStruct((64, 256), jnp.float32),
        ),
        in_specs=[vmem, vmem],
        out_specs=(vmem, vmem),
        scratch_shapes=[
            pltpu.VMEM((16, 72, 128), jnp.bfloat16),
            pltpu.VMEM((16, 72, 128), jnp.bfloat16),
            pltpu.VMEM((64, 256), jnp.float32),
            pltpu.VMEM((16, 72, 128), jnp.bfloat16),
            pltpu.VMEM((16, 8, 128), jnp.float32),
            pltpu.VMEM((32, 72, 128), jnp.bfloat16),
            pltpu.VMEM((32, 8, 128), jnp.float32),
            pltpu.VMEM((4, 72, 128), jnp.bfloat16),
            pltpu.VMEM((4, 8, 128), jnp.float32),
            pltpu.VMEM((8, 128), jnp.float32),
            pltpu.VMEM((16, 8, 128), jnp.float32),
            dma((2,)),
            dma((2,)),
            dma((2, 16)),
            dma((2, 32)),
            dma((2, 8)),
            dma((2, 4)),
            dma((16,)),
            dma((16,)),
        ],
        compiler_params=pltpu.CompilerParams(collective_id=0, has_side_effects=True),
    )(w_sum, s_sum)


def body(
    image,
    conv_kernel,
    conv_bias,
    norm_gain,
    norm_bias,
    in_weight,
    in_bias,
    out_weight,
    out_bias,
    layer_scale,
    cotangent,
):
    n_rows, n_cols, channels = image.shape
    hidden_units = in_weight.shape[1]
    factor = 1.0 / math.sqrt(n_rows * lax.axis_size("rows") * n_cols * lax.axis_size("cols"))
    sides = (("rows", 0), ("cols", 1))
    taps = conv_kernel.reshape(49, channels)
    taps = jnp.concatenate([taps, taps[:, 128:]], axis=1)
    rows = jnp.stack([conv_bias, norm_gain, norm_bias, out_bias, layer_scale])
    rows = jnp.pad(rows, ((0, 3), (0, 0)))
    padded = padded_2(image, sides, 3)
    output, d_conv, w_sum, s_sum = block(
        padded, image, cotangent, taps, rows, in_weight, in_bias, out_weight
    )
    grad_image = transposed_conv(padded_2(d_conv, sides, 3), cotangent, taps)
    w_share, s_all = reduce_all(w_sum, s_sum, factor)
    s_all = s_all[:, :channels]
    bias_all = s_all[54:58].reshape(hidden_units)
    bias_share = lax.dynamic_slice(bias_all, (lax.axis_index("rows") * SHARE,), (SHARE,))
    return (
        output,
        grad_image,
        s_all[:49].reshape(7, 7, channels),
        s_all[49],
        s_all[50],
        s_all[51],
        w_share[:, :channels].T,
        bias_share,
        w_share[:, channels:],
        s_all[52],
        s_all[53],
    )


def solution(mesh):
    placed = (
        P("rows", "cols", None),
        P(),
        P(),
        P(),
        P(),
        P(),
        P(),
        P(),
        P(),
        P(),
        P("rows", "cols", None),
    )
    return jax.shard_map(
        body,
        mesh=mesh,
        in_specs=placed,
        out_specs=(
            P("rows", "cols", None),
            P("rows", "cols", None),
            P(),
            P(),
            P(),
            P(),
            P(None, "rows"),
            P("rows"),
            P("rows", None),
            P(),
            P(),
        ),
        check_vma=False,
    )
```

```python
import functools
import math

import jax
import jax.numpy as jnp
from jax import lax
from jax.experimental import pallas as pl
from jax.experimental.pallas import tpu as pltpu
from jax.sharding import PartitionSpec as P


def gelu_parts(hidden):
    normal_cdf = 0.5 * (1.0 + jax.scipy.special.erf(hidden * 0.7071067811865476))
    normal_pdf = jnp.exp(-0.5 * hidden * hidden) * 0.3989422804014327
    return (hidden * normal_cdf, normal_cdf + hidden * normal_pdf)


MESH = pl.DeviceIdType.MESH
SHARE = 24
CHUNK = 2
VMEM_LIMIT = 64 * 1024 * 1024 - 65536
SIDES = ((-1, 0), (1, 0), (0, -1), (0, 1), (-1, -1), (-1, 1), (1, -1), (1, 1))


def remote(source, target, send, recv, place):
    return pltpu.make_async_remote_copy(
        source, target, send, recv, device_id=place, device_id_type=MESH
    )


def halo_parts(block_ref, halo, k):
    top, bottom, left, right = halo
    d_row, d_col = SIDES[k]
    first, last = pl.ds(0, 16), pl.ds(176, 16)
    if d_col == 0:
        rows = pl.ds(0, 3) if d_row < 0 else pl.ds(13, 3)
        return block_ref.at[rows], bottom if d_row < 0 else top
    cols, side = (first, right) if d_col < 0 else (last, left)
    if d_row == 0:
        return block_ref.at[:, cols], side.at[pl.ds(3, 16)]
    if d_row < 0:
        return block_ref.at[pl.ds(0, 3), cols], side.at[pl.ds(19, 3)]
    return block_ref.at[pl.ds(13, 3), cols], side.at[pl.ds(0, 3)]


def inside(row, col):
    return (row >= 0) & (row < 32) & (col >= 0) & (col < 8)


def halo_send(block_ref, halo, sems, row, col, act):
    for k, (d_row, d_col) in enumerate(SIDES):
        source, target = halo_parts(block_ref, halo, k)

        @pl.when(inside(row + d_row, col + d_col))
        def _(k=k, d_row=d_row, d_col=d_col, source=source, target=target):
            act(remote(source, target, sems.at[0, k], sems.at[1, k], (row + d_row, col + d_col)))


def halo_clear(block_ref, halo, row, col):
    for k, (d_row, d_col) in enumerate(SIDES):
        _, target = halo_parts(block_ref, halo, k)

        @pl.when(jnp.logical_not(inside(row - d_row, col - d_col)))
        def _(target=target):
            target[...] = jnp.zeros(target.shape, jnp.bfloat16)


def halo_wait(block_ref, halo, sems, row, col):
    for k, (d_row, d_col) in enumerate(SIDES):
        source, target = halo_parts(block_ref, halo, k)

        @pl.when(inside(row - d_row, col - d_col))
        def _(k=k, source=source, target=target):
            pltpu.make_async_copy(source, target, sems.at[1, k]).wait()


def widen(source_ref, main_ref, rest_ref, base):
    def step(i, carry):
        row = source_ref[i].astype(jnp.float32)
        row = jnp.concatenate(
            [jnp.zeros((3, 192), jnp.float32), row, jnp.zeros((5, 192), jnp.float32)], axis=0
        )
        main_ref[base + i] = row[:, 0:128]
        rest_ref[base + i] = jnp.concatenate([row[0:104, 128:192], row[96:200, 128:192]], axis=1)
        return carry

    lax.fori_loop(0, source_ref.shape[0], step, 0)


def join(source_ref, left_ref, right_ref, main_ref, rest_ref, base):
    def step(i, carry):
        first = jnp.concatenate(
            [
                left_ref[base + i].astype(jnp.float32)[13:16],
                source_ref[i, 0:16].astype(jnp.float32)[0:5],
            ],
            axis=0,
        )
        last = jnp.concatenate(
            [
                source_ref[i, 176:192].astype(jnp.float32)[13:16],
                right_ref[base + i].astype(jnp.float32)[0:3],
                jnp.zeros((2, 192), jnp.float32),
            ],
            axis=0,
        )
        main_ref[base + i, 0:8] = first[:, 0:128]
        main_ref[base + i, 192:200] = last[:, 0:128]
        rest_ref[base + i, 0:8, 0:64] = first[:, 128:192]
        rest_ref[base + i, 96:104, 64:128] = last[:, 128:192]
        return carry

    lax.fori_loop(0, source_ref.shape[0], step, 0)


def gather_rows(wide_ref, taps_ref, first, start, flip, accum, rows, outs):
    lo, hi = rows
    for b in range(7):
        shifted = wide_ref[lo:hi, pl.ds(start + b, 8), :]
        for a in range(7):
            tap = 48 - (7 * a + b) if flip else 7 * a + b
            begin, end = max(outs[0], lo - a), min(outs[1], hi - a)
            if begin >= end:
                continue
            part = shifted[begin + a - lo : end + a - lo] * taps_ref[tap, first : first + 128]
            part = accum[begin - outs[0] : end - outs[0]] + part
            pieces = [accum[: begin - outs[0]], part, accum[end - outs[0] :]]
            pieces = [piece for piece in pieces if piece.shape[0]]
            accum = jnp.concatenate(pieces, axis=0) if len(pieces) > 1 else pieces[0]
    return accum


def put_main(out_ref, start, rows, tile):
    out_ref[rows, pl.ds(start, 8), 0:128] = tile


def put_rest(out_ref, start, rows, tile):
    out_ref[rows, pl.ds(start, 8), 128:192] = tile[:, :, 0:64]
    out_ref[rows, pl.ds(start + 96, 8), 128:192] = tile[:, :, 64:128]


def take_main(out_ref, start, rows):
    return out_ref[rows, pl.ds(start, 8), 0:128]


def take_rest(out_ref, start, rows):
    return jnp.concatenate(
        [
            out_ref[rows, pl.ds(start, 8), 128:192],
            out_ref[rows, pl.ds(start + 96, 8), 128:192],
        ],
        axis=2,
    )


def tiles(wide_ref, taps_ref, first, flip, out_ref, put, rows, span, stride=1):
    def step(i, carry):
        start = pl.multiple_of(8 * stride * i, 8)
        accum = jnp.zeros((16, 8, 128), jnp.float32)
        accum = gather_rows(wide_ref, taps_ref, first, start, flip, accum, rows, (0, 16))
        put(out_ref, start, slice(0, 16), accum)
        return carry

    lax.fori_loop(span[0], span[1], step, 0)


def edge_rows(wide_ref, taps_ref, first, out_ref, take, put, span):
    def step(i, carry):
        start = pl.multiple_of(8 * i, 8)
        for rows, outs in (((0, 3), (0, 3)), ((19, 22), (13, 16))):
            where = slice(*outs)
            accum = take(out_ref, start, where)
            accum = gather_rows(wide_ref, taps_ref, first, start, False, accum, rows, outs)
            put(out_ref, start, where, accum)
        return carry

    lax.fori_loop(span[0], span[1], step, 0)


def tap_sums(wide_ref, d_ref, first, sums_ref, steps):
    n_rows = d_ref.shape[0]

    def step(i, carry):
        start = pl.multiple_of(8 * i, 8)
        d_tile = d_ref[:, pl.ds(start, 8), :]
        for b in range(7):
            shifted = wide_ref[:, pl.ds(start + b, 8), :]
            for a in range(7):
                tap = 7 * a + b
                sums_ref[tap, :, first : first + 128] += jnp.sum(
                    shifted[a : a + n_rows] * d_tile, axis=0
                )
        return carry

    lax.fori_loop(0, steps, step, 0)


def fold(values):
    return jnp.sum(values.reshape(values.shape[0] // 8, 8, values.shape[1]), axis=0)


def fused_kernel(
    factor,
    image_ref,
    cot_ref,
    kernel_ref,
    rows_ref,
    in_weight_ref,
    out_weight_ref,
    output_ref,
    grad_image_ref,
    g_kernel_ref,
    g_rows_ref,
    g_in_out_ref,
    g_bias_out_ref,
    g_out_out_ref,
    taps_ref,
    in_t_ref,
    out_t_ref,
    main_ref,
    rest_ref,
    conv_ref,
    d_main_ref,
    d_rest_ref,
    d_block_ref,
    top_ref,
    bottom_ref,
    left_ref,
    right_ref,
    d_top_ref,
    d_bottom_ref,
    d_left_ref,
    d_right_ref,
    sums_ref,
    tap_ref,
    bias_sum_ref,
    g_in_ref,
    g_out_ref,
    w_ref,
    s_ref,
    core_tx,
    core_rx,
    score_rx,
    row_tx,
    srow_tx,
    row_rx,
    srow_rx,
    col_rx,
    scol_rx,
    gat_tx,
    gat_rx,
    halo_sems,
    d_halo_sems,
    core_send,
    core_recv,
    row_send,
    row_recv,
    col_send,
    col_recv,
    gat_send,
    gat_recv,
):
    n_rows, n_cols, channels = image_ref.shape
    pixels = CHUNK * n_cols
    f32, bf16 = jnp.float32, jnp.bfloat16
    row = lax.axis_index("rows")
    col = lax.axis_index("cols")
    core = lax.rem(col, 2)
    pair = col - core
    other = pair + 1 - core
    half = row // 16
    place = lax.rem(row, 16)
    owner = half == core
    halo = (top_ref, bottom_ref, left_ref, right_ref)
    d_halo = (d_top_ref, d_bottom_ref, d_left_ref, d_right_ref)

    barrier = pltpu.get_barrier_semaphore()

    def greet_row(step, carry):
        peer = lax.rem(row + step, 32)
        pl.semaphore_signal(barrier, inc=1, device_id=(peer, col), device_id_type=MESH)
        return carry

    def greet_col(step, carry):
        peer = lax.rem(col + step, 8)
        pl.semaphore_signal(barrier, inc=1, device_id=(row, peer), device_id_type=MESH)
        return carry

    lax.fori_loop(1, 32, greet_row, 0)
    lax.fori_loop(1, 8, greet_col, 0)
    for d_row, d_col in SIDES[4:]:
        corner = (lax.rem(row + d_row + 32, 32), lax.rem(col + d_col + 8, 8))
        pl.semaphore_signal(barrier, inc=1, device_id=corner, device_id_type=MESH)

    halo_clear(image_ref, halo, row, col)
    halo_clear(d_block_ref, d_halo, row, col)
    for a in range(7):
        taps_ref[7 * a : 7 * a + 7, 0:192] = kernel_ref[a]
        taps_ref[7 * a : 7 * a + 7, 192:256] = kernel_ref[a][:, 128:192]
    widen(image_ref, main_ref, rest_ref, 3)
    own = (3, 19)
    tiles(rest_ref, taps_ref, 128, False, conv_ref, put_rest, own, (1, 11))
    pl.semaphore_wait(barrier, 42)
    halo_send(image_ref, halo, halo_sems, row, col, lambda copy: copy.start())
    tiles(main_ref, taps_ref, 0, False, conv_ref, put_main, own, (1, 23))
    in_t_ref[...] = in_weight_ref[...].astype(f32).T.astype(bf16)
    out_t_ref[...] = out_weight_ref[...].astype(f32).T.astype(bf16)
    sums_ref[...] = jnp.zeros_like(sums_ref)
    tap_ref[...] = jnp.zeros_like(tap_ref)
    bias_sum_ref[...] = jnp.zeros_like(bias_sum_ref)
    g_in_ref[...] = jnp.zeros_like(g_in_ref)
    g_out_ref[...] = jnp.zeros_like(g_out_ref)
    s_ref[...] = jnp.zeros_like(s_ref)
    halo_wait(image_ref, halo, halo_sems, row, col)

    def widen_all(block_ref, pieces, center):
        above, below, left, right = pieces
        for source, base in ((above, 0), (below, 19)) + (((block_ref, 3),) if center else ()):
            widen(source, main_ref, rest_ref, base)
        for source, base in ((above, 0), (block_ref, 3), (below, 19)):
            join(source, left, right, main_ref, rest_ref, base)

    widen_all(image_ref, halo, False)
    whole = (0, 22)
    edge_rows(main_ref, taps_ref, 0, conv_ref, take_main, put_main, (1, 23))
    edge_rows(rest_ref, taps_ref, 128, conv_ref, take_rest, put_rest, (1, 11))
    tiles(main_ref, taps_ref, 0, False, conv_ref, put_main, whole, (0, 2), 23)
    tiles(rest_ref, taps_ref, 128, False, conv_ref, put_rest, whole, (0, 2), 11)

    def chunk(i, carry):
        span = pl.ds(CHUNK * i, CHUNK)
        conv_bias, gain, norm_bias, out_bias, layer_scale = (
            rows_ref[k : k + 1, 0:channels] for k in range(5)
        )
        conv_out = conv_ref[span].reshape(pixels, channels) + conv_bias
        centred = conv_out - jnp.mean(conv_out, axis=-1, keepdims=True)
        inv_std = lax.rsqrt(jnp.mean(centred * centred, axis=-1, keepdims=True) + 1e-06)
        unit_norm = centred * inv_std
        normed = (unit_norm * gain + norm_bias).astype(bf16)
        hidden = jnp.dot(normed, in_weight_ref[...], preferred_element_type=f32) + rows_ref[5:6]
        act_full, gelu_slope = gelu_parts(hidden)
        activation = act_full.astype(bf16)
        branch = jnp.dot(activation, out_weight_ref[...], preferred_element_type=f32) + out_bias
        centre = image_ref[span].astype(f32).reshape(pixels, channels)
        output_ref[span] = (
            (centre + layer_scale * branch).astype(bf16).reshape(CHUNK, n_cols, channels)
        )
        cot_full = cot_ref[span].astype(f32).reshape(pixels, channels)
        scaled = (cot_full * layer_scale).astype(bf16)
        d_act = jnp.dot(scaled, out_t_ref[...], preferred_element_type=f32)
        d_hidden_full = d_act * gelu_slope
        d_hidden = d_hidden_full.astype(bf16)
        d_normed = jnp.dot(d_hidden, in_t_ref[...], preferred_element_type=f32)
        d_unit = d_normed * gain
        d_conv = (
            d_unit
            - jnp.mean(d_unit, axis=-1, keepdims=True)
            - unit_norm * jnp.mean(d_unit * unit_norm, axis=-1, keepdims=True)
        ) * inv_std
        d_conv_3 = d_conv.reshape(CHUNK, n_cols, channels)
        d_main_ref[span] = d_conv_3[:, :, 0:128]
        d_rest_ref[span] = jnp.concatenate(
            [d_conv_3[:, 0:96, 128:192], d_conv_3[:, 96:192, 128:192]], axis=2
        )
        d_block_ref[span] = d_conv_3.astype(bf16)
        contract = (((0,), (0,)), ((), ()))
        g_in_ref[...] += lax.dot_general(normed, d_hidden, contract, preferred_element_type=f32)
        g_out_ref[...] += lax.dot_general(scaled, activation, contract, preferred_element_type=f32)
        bias_sum_ref[...] += fold(d_hidden_full)
        sums_ref[0] += fold(d_conv)
        sums_ref[1] += fold(d_normed * unit_norm)
        sums_ref[2] += fold(d_normed)
        sums_ref[3] += fold(cot_full)
        sums_ref[4] += fold(cot_full * branch)
        return carry

    lax.fori_loop(0, n_rows // CHUNK, chunk, 0)
    halo_send(d_block_ref, d_halo, d_halo_sems, row, col, lambda copy: copy.start())

    w_ref[:, 0:channels] = g_in_ref[...].T
    w_ref[:, channels : 2 * channels] = g_out_ref[...].T

    def share_of(index):
        rows = w_ref[pl.ds(pl.multiple_of(index * SHARE, 8), SHARE), :]
        return jnp.concatenate([rows[:, 0:128], rows[:, 128:256], rows[:, 256:384]], axis=0)

    def pack_core(j, carry):
        core_tx[j] = share_of(16 * (1 - core) + j).astype(bf16)
        return carry

    lax.fori_loop(0, 16, pack_core, 0)
    to_core = remote(core_tx, core_rx, core_send.at[0], core_recv.at[0], (row, other))
    to_core_s = remote(s_ref, score_rx, core_send.at[1], core_recv.at[1], (row, other))
    to_core.start()

    tap_sums(rest_ref, d_rest_ref, 128, tap_ref, 12)
    to_core.wait()

    def row_copy(j):
        return remote(
            row_tx.at[j],
            row_rx.at[row],
            row_send.at[0, j],
            row_recv.at[0, row],
            (16 * core + j, col),
        )

    def s_row_copy(j):
        return remote(
            srow_tx.at[j],
            srow_rx.at[row],
            row_send.at[1, j],
            row_recv.at[1, row],
            (16 * core + j, col),
        )

    def col_copy(step):
        return remote(
            col_rx.at[col // 2],
            col_rx.at[col // 2],
            col_send.at[0, step],
            col_recv.at[0, col // 2],
            (row, lax.rem(col + step, 8)),
        )

    def s_col_copy(step):
        return remote(
            scol_rx.at[col // 2],
            scol_rx.at[col // 2],
            col_send.at[1, step],
            col_recv.at[1, col // 2],
            (row, lax.rem(col + step, 8)),
        )

    def gather_copy(step):
        peer = 16 * half + lax.rem(place + step, 16)
        return remote(
            gat_tx, gat_rx.at[place], gat_send.at[step], gat_recv.at[place], (peer, col)
        )

    def over_rows(act):
        def step(k, carry):
            j = lax.rem(place + k, 16)

            @pl.when(16 * core + j != row)
            def _():
                act(j)

            return carry

        lax.fori_loop(0, 16, step, 0)

    def over(first, last, act):
        def step(k, carry):
            act(k)
            return carry

        lax.fori_loop(first, last, step, 0)

    def pack_row(j, carry):
        row_tx[j] = (share_of(16 * core + j) + core_rx[j].astype(f32)).astype(bf16)
        return carry

    lax.fori_loop(0, 16, pack_row, 0)
    over_rows(lambda j: row_copy(j).start())

    tap_sums(main_ref, d_main_ref, 0, tap_ref, 24)
    taps = jnp.sum(tap_ref[...], axis=1)
    s_ref[0:49, 0:128] = taps[:, 0:128]
    s_ref[0:49, 128:192] = taps[:, 128:192] + taps[:, 192:256]
    s_ref[49:54, 0:channels] = jnp.sum(sums_ref[...], axis=1)
    s_ref[52:53, 0:channels] = s_ref[52:53, 0:channels] * rows_ref[4:5, 0:channels]
    bias_sum = jnp.sum(bias_sum_ref[...], axis=0, keepdims=True)
    for k in range(4):
        s_ref[54 + k : 55 + k, 0:channels] = bias_sum[:, channels * k : channels * (k + 1)]
    to_core_s.start()

    halo_wait(d_block_ref, d_halo, d_halo_sems, row, col)
    widen_all(d_block_ref, d_halo, True)
    tiles(rest_ref, taps_ref, 128, True, conv_ref, put_rest, whole, (0, 6))

    to_core_s.wait()
    for j in range(16):
        up, across = 8 * (j // 2), 128 * (j % 2)
        srow_tx[j] = (
            s_ref[up : up + 8, across : across + 128]
            + score_rx[up : up + 8, across : across + 128]
        )
    over_rows(lambda j: s_row_copy(j).start())

    @pl.when(owner)
    def _():
        row_rx[row] = row_tx[place]

        def wait_row(step):
            peer = lax.rem(row + step, 32)
            pltpu.make_async_copy(row_tx.at[0], row_rx.at[peer], row_recv.at[0, peer]).wait()

        over(1, 32, wait_row)

        def add_row(i, carry):
            return carry + row_rx[i].astype(f32)

        total = lax.fori_loop(0, 32, add_row, jnp.zeros((72, 128), f32))
        col_rx[col // 2] = total.astype(bf16)
        over(1, 8, lambda step: col_copy(step).start())

    tiles(main_ref, taps_ref, 0, True, conv_ref, put_main, whole, (0, 12))

    @pl.when(owner)
    def _():
        srow_rx[row] = srow_tx[place]

        def wait_row(step):
            peer = lax.rem(row + step, 32)
            pltpu.make_async_copy(srow_tx.at[0], srow_rx.at[peer], row_recv.at[1, peer]).wait()

        over(1, 32, wait_row)

        def add_row(i, carry):
            return carry + srow_rx[i]

        scol_rx[col // 2] = lax.fori_loop(0, 32, add_row, jnp.zeros((8, 128), f32))
        over(1, 8, lambda step: s_col_copy(step).start())

    tiles(main_ref, taps_ref, 0, True, conv_ref, put_main, whole, (12, 18))

    def wait_col(y):
        @pl.when(2 * y + half != col)
        def _():
            pltpu.make_async_copy(scol_rx.at[y], scol_rx.at[y], col_recv.at[1, y]).wait()

    over(0, 4, wait_col)
    gat_tx[...] = ((scol_rx[0] + scol_rx[1]) + (scol_rx[2] + scol_rx[3])) * factor
    over(1, 16, lambda step: gather_copy(step).start())

    tiles(main_ref, taps_ref, 0, True, conv_ref, put_main, whole, (18, 24))
    tiles(rest_ref, taps_ref, 128, True, conv_ref, put_rest, whole, (6, 12))

    def finish(i, carry):
        grad_image_ref[i] = (cot_ref[i].astype(f32) + conv_ref[i]).astype(bf16)
        return carry

    lax.fori_loop(0, n_rows, finish, 0)

    def wait_share(y):
        @pl.when(2 * y + half != col)
        def _():
            pltpu.make_async_copy(col_rx.at[y], col_rx.at[y], col_recv.at[0, y]).wait()

    over(0, 4, wait_share)
    share = jnp.zeros((72, 128), f32)
    for y in range(4):
        share = share + col_rx[y].astype(f32)
    share = share * factor
    share = jnp.concatenate([share[0:24], share[24:48], share[48:72]], axis=1)
    g_in_out_ref[...] = share[:, 0:channels].T
    g_out_out_ref[...] = share[:, channels : 2 * channels]

    gat_rx[place] = gat_tx[...]

    def wait_gather(step):
        peer = lax.rem(place + step, 16)
        pltpu.make_async_copy(gat_tx, gat_rx.at[peer], gat_recv.at[peer]).wait()

    over(1, 16, wait_gather)
    for j in range(16):
        up, across = 8 * (j // 2), 128 * (j % 2)
        score_rx[up : up + 8, across : across + 128] = gat_rx[j]
    for a in range(7):
        g_kernel_ref[a] = score_rx[7 * a : 7 * a + 7, 0:channels]
    g_rows_ref[...] = score_rx[48:56, 0:channels]
    picked = jnp.zeros((1, 256), f32)
    for k in range(4):
        picked = picked + jnp.where(row // 8 == k, score_rx[54 + k : 55 + k, :], 0.0)
    picked = pltpu.roll(
        jnp.broadcast_to(picked, (8, 256)), lax.rem(256 - SHARE * lax.rem(row, 8), 256), 1
    )
    g_bias_out_ref[...] = picked[0:1, 0:SHARE]

    halo_send(image_ref, halo, halo_sems, row, col, lambda copy: copy.wait_send())
    halo_send(d_block_ref, d_halo, d_halo_sems, row, col, lambda copy: copy.wait_send())
    over_rows(lambda j: row_copy(j).wait_send())
    over_rows(lambda j: s_row_copy(j).wait_send())

    @pl.when(owner)
    def _():
        over(1, 8, lambda step: col_copy(step).wait_send())
        over(1, 8, lambda step: s_col_copy(step).wait_send())

    over(1, 16, lambda step: gather_copy(step).wait_send())


def fused(image, cotangent, conv_kernel, rows, in_weight, out_weight, factor):
    n_rows, n_cols, channels = image.shape
    hidden_units = in_weight.shape[1]
    vmem = pl.BlockSpec(memory_space=pltpu.VMEM)
    dma = pltpu.SemaphoreType.DMA
    f32, bf16 = jnp.float32, jnp.bfloat16
    halo = [
        pltpu.VMEM((3, n_cols, channels), bf16),
        pltpu.VMEM((3, n_cols, channels), bf16),
        pltpu.VMEM((n_rows + 6, 16, channels), bf16),
        pltpu.VMEM((n_rows + 6, 16, channels), bf16),
    ]
    return pl.pallas_call(
        functools.partial(fused_kernel, factor),
        out_shape=(
            jax.ShapeDtypeStruct(image.shape, bf16),
            jax.ShapeDtypeStruct(image.shape, bf16),
            jax.ShapeDtypeStruct((7, 7, channels), f32),
            jax.ShapeDtypeStruct((8, channels), f32),
            jax.ShapeDtypeStruct((channels, SHARE), f32),
            jax.ShapeDtypeStruct((1, SHARE), f32),
            jax.ShapeDtypeStruct((SHARE, channels), f32),
        ),
        in_specs=[vmem] * 6,
        out_specs=(vmem,) * 7,
        scratch_shapes=[
            pltpu.VMEM((56, 256), f32),
            pltpu.VMEM((hidden_units, channels), bf16),
            pltpu.VMEM((channels, hidden_units), bf16),
            pltpu.VMEM((n_rows + 6, 200, 128), f32),
            pltpu.VMEM((n_rows + 6, 104, 128), f32),
            pltpu.VMEM((n_rows, n_cols, channels), f32),
            pltpu.VMEM((n_rows, n_cols, 128), f32),
            pltpu.VMEM((n_rows, n_cols // 2, 128), f32),
            pltpu.VMEM((n_rows, n_cols, channels), bf16),
            *halo,
            *halo,
            pltpu.VMEM((5, 8, channels), f32),
            pltpu.VMEM((49, 8, 256), f32),
            pltpu.VMEM((8, hidden_units), f32),
            pltpu.VMEM((channels, hidden_units), f32),
            pltpu.VMEM((channels, hidden_units), f32),
            pltpu.VMEM((hidden_units, 2 * channels), f32),
            pltpu.VMEM((64, 256), f32),
            pltpu.VMEM((16, 72, 128), bf16),
            pltpu.VMEM((16, 72, 128), bf16),
            pltpu.VMEM((64, 256), f32),
            pltpu.VMEM((16, 72, 128), bf16),
            pltpu.VMEM((16, 8, 128), f32),
            pltpu.VMEM((32, 72, 128), bf16),
            pltpu.VMEM((32, 8, 128), f32),
            pltpu.VMEM((4, 72, 128), bf16),
            pltpu.VMEM((4, 8, 128), f32),
            pltpu.VMEM((8, 128), f32),
            pltpu.VMEM((16, 8, 128), f32),
            dma((2, 8)),
            dma((2, 8)),
            dma((2,)),
            dma((2,)),
            dma((2, 16)),
            dma((2, 32)),
            dma((2, 8)),
            dma((2, 4)),
            dma((16,)),
            dma((16,)),
        ],
        compiler_params=pltpu.CompilerParams(
            collective_id=0, has_side_effects=True, vmem_limit_bytes=VMEM_LIMIT
        ),
    )(image, cotangent, conv_kernel, rows, in_weight, out_weight)


def body(
    image,
    conv_kernel,
    conv_bias,
    norm_gain,
    norm_bias,
    in_weight,
    in_bias,
    out_weight,
    out_bias,
    layer_scale,
    cotangent,
):
    n_rows, n_cols, channels = image.shape
    hidden_units = in_weight.shape[1]
    factor = 1.0 / math.sqrt(n_rows * lax.axis_size("rows") * n_cols * lax.axis_size("cols"))
    rows = jnp.stack([conv_bias, norm_gain, norm_bias, out_bias, layer_scale])
    rows = jnp.pad(rows, ((0, 0), (0, hidden_units - channels)))
    rows = jnp.concatenate([rows, in_bias[None], jnp.zeros((2, hidden_units), jnp.float32)], axis=0)
    output, grad_image, g_kernel, g_rows, g_in, g_bias, g_out = fused(
        image, cotangent, conv_kernel, rows, in_weight, out_weight, factor
    )
    return (
        output,
        grad_image,
        g_kernel,
        g_rows[1],
        g_rows[2],
        g_rows[3],
        g_in,
        g_bias[0],
        g_out,
        g_rows[4],
        g_rows[5],
    )


def solution(mesh):
    placed = (
        P("rows", "cols", None),
        P(),
        P(),
        P(),
        P(),
        P(),
        P(),
        P(),
        P(),
        P(),
        P("rows", "cols", None),
    )
    return jax.shard_map(
        body,
        mesh=mesh,
        in_specs=placed,
        out_specs=(
            P("rows", "cols", None),
            P("rows", "cols", None),
            P(),
            P(),
            P(),
            P(),
            P(None, "rows"),
            P("rows"),
            P("rows", None),
            P(),
            P(),
        ),
        check_vma=False,
    )
```

```python
import functools
import math

import jax
import jax.numpy as jnp
from jax import lax
from jax.experimental import pallas as pl
from jax.experimental.pallas import tpu as pltpu
from jax.sharding import PartitionSpec as P


def gelu_parts(hidden):
    normal_cdf = 0.5 * (1.0 + jax.scipy.special.erf(hidden * 0.7071067811865476))
    normal_pdf = jnp.exp(-0.5 * hidden * hidden) * 0.3989422804014327
    return (hidden * normal_cdf, normal_cdf + hidden * normal_pdf)


MESH = pl.DeviceIdType.MESH
SHARE = 24
CHUNK = 2
VMEM_LIMIT = 50 * 1024 * 1024
SIDES = ((-1, 0), (1, 0), (0, -1), (0, 1), (-1, -1), (-1, 1), (1, -1), (1, 1))


def remote(source, target, send, recv, place):
    return pltpu.make_async_remote_copy(
        source, target, send, recv, device_id=place, device_id_type=MESH
    )


def halo_parts(block_ref, halo, k):
    top, bottom, left, right = halo
    d_row, d_col = SIDES[k]
    first, last = pl.ds(0, 16), pl.ds(176, 16)
    if d_col == 0:
        rows = pl.ds(0, 3) if d_row < 0 else pl.ds(13, 3)
        return block_ref.at[rows], bottom if d_row < 0 else top
    cols, side = (first, right) if d_col < 0 else (last, left)
    if d_row == 0:
        return block_ref.at[:, cols], side.at[pl.ds(3, 16)]
    if d_row < 0:
        return block_ref.at[pl.ds(0, 3), cols], side.at[pl.ds(19, 3)]
    return block_ref.at[pl.ds(13, 3), cols], side.at[pl.ds(0, 3)]


def inside(row, col):
    return (row >= 0) & (row < 32) & (col >= 0) & (col < 8)


def halo_send(block_ref, halo, sems, row, col, act):
    for k, (d_row, d_col) in enumerate(SIDES):
        source, target = halo_parts(block_ref, halo, k)

        @pl.when(inside(row + d_row, col + d_col))
        def _(k=k, d_row=d_row, d_col=d_col, source=source, target=target):
            act(remote(source, target, sems.at[0, k], sems.at[1, k], (row + d_row, col + d_col)))


def halo_clear(block_ref, halo, row, col):
    for k, (d_row, d_col) in enumerate(SIDES):
        _, target = halo_parts(block_ref, halo, k)

        @pl.when(jnp.logical_not(inside(row - d_row, col - d_col)))
        def _(target=target):
            target[...] = jnp.zeros(target.shape, jnp.bfloat16)


def halo_wait(block_ref, halo, sems, row, col):
    for k, (d_row, d_col) in enumerate(SIDES):
        source, target = halo_parts(block_ref, halo, k)

        @pl.when(inside(row - d_row, col - d_col))
        def _(k=k, source=source, target=target):
            pltpu.make_async_copy(source, target, sems.at[1, k]).wait()


def widen(source_ref, main_ref, rest_ref, base):
    def step(i, carry):
        row = source_ref[i].astype(jnp.float32)
        row = jnp.concatenate(
            [jnp.zeros((3, 192), jnp.float32), row, jnp.zeros((5, 192), jnp.float32)], axis=0
        )
        main_ref[base + i] = row[:, 0:128]
        rest_ref[base + i] = jnp.concatenate([row[0:104, 128:192], row[96:200, 128:192]], axis=1)
        return carry

    lax.fori_loop(0, source_ref.shape[0], step, 0)


def join(source_ref, left_ref, right_ref, main_ref, rest_ref, base):
    def step(i, carry):
        first = jnp.concatenate(
            [
                left_ref[base + i].astype(jnp.float32)[13:16],
                source_ref[i, 0:16].astype(jnp.float32)[0:5],
            ],
            axis=0,
        )
        last = jnp.concatenate(
            [
                source_ref[i, 176:192].astype(jnp.float32)[13:16],
                right_ref[base + i].astype(jnp.float32)[0:3],
                jnp.zeros((2, 192), jnp.float32),
            ],
            axis=0,
        )
        main_ref[base + i, 0:8] = first[:, 0:128]
        main_ref[base + i, 192:200] = last[:, 0:128]
        rest_ref[base + i, 0:8, 0:64] = first[:, 128:192]
        rest_ref[base + i, 96:104, 64:128] = last[:, 128:192]
        return carry

    lax.fori_loop(0, source_ref.shape[0], step, 0)


def gather_rows(wide_ref, taps_ref, first, start, flip, accum, rows, outs):
    lo, hi = rows
    for b in range(7):
        shifted = wide_ref[lo:hi, pl.ds(start + b, 8), :]
        for a in range(7):
            tap = 48 - (7 * a + b) if flip else 7 * a + b
            begin, end = max(outs[0], lo - a), min(outs[1], hi - a)
            if begin >= end:
                continue
            part = shifted[begin + a - lo : end + a - lo] * taps_ref[tap, first : first + 128]
            part = accum[begin - outs[0] : end - outs[0]] + part
            pieces = [accum[: begin - outs[0]], part, accum[end - outs[0] :]]
            pieces = [piece for piece in pieces if piece.shape[0]]
            accum = jnp.concatenate(pieces, axis=0) if len(pieces) > 1 else pieces[0]
    return accum


def put_main(out_ref, start, rows, tile):
    out_ref[rows, pl.ds(start, 8), 0:128] = tile


def put_rest(out_ref, start, rows, tile):
    out_ref[rows, pl.ds(start, 8), 128:192] = tile[:, :, 0:64]
    out_ref[rows, pl.ds(start + 96, 8), 128:192] = tile[:, :, 64:128]


def take_main(out_ref, start, rows):
    return out_ref[rows, pl.ds(start, 8), 0:128]


def take_rest(out_ref, start, rows):
    return jnp.concatenate(
        [
            out_ref[rows, pl.ds(start, 8), 128:192],
            out_ref[rows, pl.ds(start + 96, 8), 128:192],
        ],
        axis=2,
    )


def tiles(wide_ref, taps_ref, first, flip, out_ref, put, rows, span, stride=1):
    def step(i, carry):
        start = pl.multiple_of(8 * stride * i, 8)
        accum = jnp.zeros((16, 8, 128), jnp.float32)
        accum = gather_rows(wide_ref, taps_ref, first, start, flip, accum, rows, (0, 16))
        put(out_ref, start, slice(0, 16), accum)
        return carry

    lax.fori_loop(span[0], span[1], step, 0)


def edge_rows(wide_ref, taps_ref, first, out_ref, take, put, span):
    def step(i, carry):
        start = pl.multiple_of(8 * i, 8)
        for rows, outs in (((0, 3), (0, 3)), ((19, 22), (13, 16))):
            where = slice(*outs)
            accum = take(out_ref, start, where)
            accum = gather_rows(wide_ref, taps_ref, first, start, False, accum, rows, outs)
            put(out_ref, start, where, accum)
        return carry

    lax.fori_loop(span[0], span[1], step, 0)


def split_taps(taps_ref, parts_ref, flip):
    row = [taps_ref[7 * a : 7 * a + 7, :] for a in (range(6, -1, -1) if flip else range(7))]
    groups = (
        (row[0], row[2], row[4], row[6]),
        (row[0] + row[1], row[2] + row[3], row[4] + row[5], row[6]),
        (row[1], row[3], row[5], jnp.zeros_like(row[0])),
    )
    for g, taps in enumerate(groups):
        for j in range(2):
            even, odd = taps[2 * j], taps[2 * j + 1]
            for q, part in enumerate((even, even + odd, odd)):
                parts_ref[(3 * g + q) * 2 + j, 0:7] = part


def split_rows(wide_ref, parts_ref):
    def step(i, carry):
        at = pl.ds(pl.multiple_of(8 * i, 8), 8)
        x = [wide_ref[r, at, :] for r in range(22)]
        groups = (
            [x[2 * m] - x[2 * m + 1] for m in range(11)],
            [x[2 * m + 1] for m in range(11)],
            [x[2 * m + 2] - x[2 * m + 1] for m in range(10)],
        )
        for g, s in enumerate(groups):
            for n in range(5):
                parts_ref[15 * g + n, at, :] = s[2 * n] - s[2 * n + 1]
                parts_ref[15 * g + 5 + n, at, :] = s[2 * n + 1]
                if 2 * n + 2 < len(s):
                    parts_ref[15 * g + 10 + n, at, :] = s[2 * n + 2] - s[2 * n + 1]
        return carry

    lax.fori_loop(0, wide_ref.shape[1] // 8, step, 0)


def part_terms():
    return [(g, q, j) for g in range(3) for q in range(3) for j in range(2) if (g, q, j) != (2, 2, 1)]


def part_rows(parts_ref, start):
    counts = [5] * 8 + [4]
    return [parts_ref[5 * k : 5 * k + n, pl.ds(start, 8), :] for k, n in enumerate(counts)]


def part_tile(parts_ref, taps_ref, first, start, flip):
    accum = [None] * 9
    for b in range(7):
        rows = part_rows(parts_ref, start + b)
        for g, q, j in part_terms():
            k = 3 * g + q
            tap = 6 - b if flip else b
            term = rows[k][j : j + 4] * taps_ref[2 * k + j, tap : tap + 1, first : first + 128]
            accum[k] = term if accum[k] is None else accum[k] + term
    even = [accum[3 * g] + accum[3 * g + 1] for g in range(3)]
    odd = [accum[3 * g + 1] + accum[3 * g + 2] for g in range(3)]
    out = []
    for n in range(4):
        for p in (even, odd):
            out.append(p[0][n : n + 1] + p[1][n : n + 1])
            out.append(p[1][n : n + 1] + p[2][n : n + 1])
    return jnp.concatenate(out, axis=0)


def tap_sums(parts_ref, d_ref, first, sums_ref, steps):
    def step(i, carry):
        start = pl.multiple_of(8 * i, 8)
        d = [d_ref[r, pl.ds(start, 8), :] for r in range(16)]
        even, odd = d[0::2], d[1::2]
        vectors = []
        for v in (even, [a + b for a, b in zip(even, odd)], odd):
            v_even, v_odd = v[0::2], v[1::2]
            vectors += [v_even, [a + b for a, b in zip(v_even, v_odd)], v_odd]
        vectors = [jnp.stack(v) for v in vectors]
        for b in range(7):
            dots = {}
            rows = part_rows(parts_ref, start + b)
            for g, q, j in part_terms():
                k = 3 * g + q
                dots[g, q, j] = jnp.sum(rows[k][j : j + 4] * vectors[k], axis=0)
            p = {}
            for g in range(3):
                for j in range(2):
                    p[g, 2 * j] = dots[g, 0, j] + dots[g, 1, j]
                    if (g, j) != (2, 1):
                        p[g, 2 * j + 1] = dots[g, 1, j] + dots[g, 2, j]
            for i in range(4):
                sums_ref[14 * i + b, :, first : first + 128] += p[0, i] + p[1, i]
                if i < 3:
                    sums_ref[14 * i + 7 + b, :, first : first + 128] += p[1, i] + p[2, i]
        return carry

    lax.fori_loop(0, steps, step, 0)


def part_tiles(parts_ref, taps_ref, first, out_ref, put, span):
    def step(i, carry):
        start = pl.multiple_of(8 * i, 8)
        put(out_ref, start, slice(0, 16), part_tile(parts_ref, taps_ref, first, start, True))
        return carry

    lax.fori_loop(span[0], span[1], step, 0)


def fold(values):
    return jnp.sum(values.reshape(values.shape[0] // 8, 8, values.shape[1]), axis=0)


def fused_kernel(
    factor,
    image_ref,
    cot_hbm_ref,
    kernel_ref,
    conv_bias_ref,
    gain_ref,
    norm_bias_ref,
    out_bias_ref,
    layer_scale_ref,
    in_bias_ref,
    in_weight_ref,
    out_t_ref,
    output_ref,
    grad_image_ref,
    g_kernel_ref,
    g_rows_ref,
    g_in_out_ref,
    g_bias_out_ref,
    g_out_out_ref,
    cot_ref,
    taps_ref,
    in_t_ref,
    out_weight_ref,
    main_ref,
    rest_ref,
    pmain_ref,
    prest_ref,
    ptaps_ref,
    conv_ref,
    d_main_ref,
    d_rest_ref,
    d_block_ref,
    top_ref,
    bottom_ref,
    left_ref,
    right_ref,
    d_top_ref,
    d_bottom_ref,
    d_left_ref,
    d_right_ref,
    sums_ref,
    tap_ref,
    bias_sum_ref,
    g_in_ref,
    g_out_ref,
    w_ref,
    s_ref,
    core_tx,
    core_rx,
    score_rx,
    row_tx,
    srow_tx,
    row_rx,
    srow_rx,
    col_rx,
    scol_rx,
    gat_tx,
    gat_rx,
    halo_sems,
    d_halo_sems,
    core_send,
    core_recv,
    row_send,
    row_recv,
    col_send,
    col_recv,
    gat_send,
    gat_recv,
    cot_sem,
):
    n_rows, n_cols, channels = image_ref.shape
    pixels = CHUNK * n_cols
    f32, bf16 = jnp.float32, jnp.bfloat16
    row = lax.axis_index("rows")
    col = lax.axis_index("cols")
    core = lax.rem(col, 2)
    pair = col - core
    other = pair + 1 - core
    half = row // 16
    place = lax.rem(row, 16)
    owner = half == core
    halo = (top_ref, bottom_ref, left_ref, right_ref)
    d_halo = (d_top_ref, d_bottom_ref, d_left_ref, d_right_ref)

    cot_copy = pltpu.make_async_copy(cot_hbm_ref, cot_ref, cot_sem)
    cot_copy.start()
    barrier = pltpu.get_barrier_semaphore()

    def greet_row(step, carry):
        peer = lax.rem(row + step, 32)
        pl.semaphore_signal(barrier, inc=1, device_id=(peer, col), device_id_type=MESH)
        return carry

    def greet_col(step, carry):
        peer = lax.rem(col + step, 8)
        pl.semaphore_signal(barrier, inc=1, device_id=(row, peer), device_id_type=MESH)
        return carry

    lax.fori_loop(1, 32, greet_row, 0)
    lax.fori_loop(1, 8, greet_col, 0)
    for d_row, d_col in SIDES[4:]:
        corner = (lax.rem(row + d_row + 32, 32), lax.rem(col + d_col + 8, 8))
        pl.semaphore_signal(barrier, inc=1, device_id=corner, device_id_type=MESH)

    halo_clear(image_ref, halo, row, col)
    halo_clear(d_block_ref, d_halo, row, col)
    for a in range(7):
        taps_ref[7 * a : 7 * a + 7, 0:192] = kernel_ref[a]
        taps_ref[7 * a : 7 * a + 7, 192:256] = kernel_ref[a][:, 128:192]
    widen(image_ref, main_ref, rest_ref, 3)
    own = (3, 19)
    tiles(rest_ref, taps_ref, 128, False, conv_ref, put_rest, own, (1, 11))
    pl.semaphore_wait(barrier, 42)
    halo_send(image_ref, halo, halo_sems, row, col, lambda copy: copy.start())
    tiles(main_ref, taps_ref, 0, False, conv_ref, put_main, own, (1, 23))
    in_t_ref[...] = in_weight_ref[...].astype(f32).T.astype(bf16)
    out_weight_ref[...] = out_t_ref[...].astype(f32).T.astype(bf16)
    sums_ref[...] = jnp.zeros_like(sums_ref)
    tap_ref[...] = jnp.zeros_like(tap_ref)
    bias_sum_ref[...] = jnp.zeros_like(bias_sum_ref)
    g_in_ref[...] = jnp.zeros_like(g_in_ref)
    g_out_ref[...] = jnp.zeros_like(g_out_ref)
    s_ref[...] = jnp.zeros_like(s_ref)
    cot_copy.wait()
    halo_wait(image_ref, halo, halo_sems, row, col)

    def widen_all(block_ref, pieces, center):
        above, below, left, right = pieces
        for source, base in ((above, 0), (below, 19)) + (((block_ref, 3),) if center else ()):
            widen(source, main_ref, rest_ref, base)
        for source, base in ((above, 0), (block_ref, 3), (below, 19)):
            join(source, left, right, main_ref, rest_ref, base)

    widen_all(image_ref, halo, False)
    whole = (0, 22)
    edge_rows(main_ref, taps_ref, 0, conv_ref, take_main, put_main, (1, 23))
    edge_rows(rest_ref, taps_ref, 128, conv_ref, take_rest, put_rest, (1, 11))
    tiles(main_ref, taps_ref, 0, False, conv_ref, put_main, whole, (0, 2), 23)
    tiles(rest_ref, taps_ref, 128, False, conv_ref, put_rest, whole, (0, 2), 11)

    split_taps(taps_ref, ptaps_ref, True)
    split_rows(main_ref, pmain_ref)
    split_rows(rest_ref, prest_ref)

    def chunk(i, carry):
        span = pl.ds(CHUNK * i, CHUNK)
        conv_bias, gain, norm_bias = conv_bias_ref[...], gain_ref[...], norm_bias_ref[...]
        out_bias, layer_scale = out_bias_ref[...], layer_scale_ref[...]
        conv_out = conv_ref[span].reshape(pixels, channels) + conv_bias
        centred = conv_out - jnp.mean(conv_out, axis=-1, keepdims=True)
        inv_std = lax.rsqrt(jnp.mean(centred * centred, axis=-1, keepdims=True) + 1e-06)
        unit_norm = centred * inv_std
        normed = (unit_norm * gain + norm_bias).astype(bf16)
        hidden = jnp.dot(normed, in_weight_ref[...], preferred_element_type=f32) + in_bias_ref[...]
        act_full, gelu_slope = gelu_parts(hidden)
        activation = act_full.astype(bf16)
        branch = jnp.dot(activation, out_weight_ref[...], preferred_element_type=f32) + out_bias
        centre = image_ref[span].astype(f32).reshape(pixels, channels)
        output_ref[span] = (
            (centre + layer_scale * branch).astype(bf16).reshape(CHUNK, n_cols, channels)
        )
        cot_full = cot_ref[span].astype(f32).reshape(pixels, channels)
        scaled = (cot_full * layer_scale).astype(bf16)
        d_act = jnp.dot(scaled, out_t_ref[...], preferred_element_type=f32)
        d_hidden_full = d_act * gelu_slope
        d_hidden = d_hidden_full.astype(bf16)
        d_normed = jnp.dot(d_hidden, in_t_ref[...], preferred_element_type=f32)
        d_unit = d_normed * gain
        d_conv = (
            d_unit
            - jnp.mean(d_unit, axis=-1, keepdims=True)
            - unit_norm * jnp.mean(d_unit * unit_norm, axis=-1, keepdims=True)
        ) * inv_std
        d_conv_3 = d_conv.reshape(CHUNK, n_cols, channels)
        d_main_ref[span] = d_conv_3[:, :, 0:128]
        d_rest_ref[span] = jnp.concatenate(
            [d_conv_3[:, 0:96, 128:192], d_conv_3[:, 96:192, 128:192]], axis=2
        )
        d_block_ref[span] = d_conv_3.astype(bf16)
        contract = (((0,), (0,)), ((), ()))
        g_in_ref[...] += lax.dot_general(normed, d_hidden, contract, preferred_element_type=f32)
        g_out_ref[...] += lax.dot_general(scaled, activation, contract, preferred_element_type=f32)
        bias_sum_ref[...] += fold(d_hidden_full)
        sums_ref[0] += fold(d_conv)
        sums_ref[1] += fold(d_normed * unit_norm)
        sums_ref[2] += fold(d_normed)
        sums_ref[3] += fold(cot_full)
        sums_ref[4] += fold(cot_full * branch)
        return carry

    lax.fori_loop(0, n_rows // CHUNK, chunk, 0)
    halo_send(d_block_ref, d_halo, d_halo_sems, row, col, lambda copy: copy.start())

    w_ref[:, 0:channels] = g_in_ref[...].T
    w_ref[:, channels : 2 * channels] = g_out_ref[...].T

    def share_of(index):
        rows = w_ref[pl.ds(pl.multiple_of(index * SHARE, 8), SHARE), :]
        return jnp.concatenate([rows[:, 0:128], rows[:, 128:256], rows[:, 256:384]], axis=0)

    def pack_core(j, carry):
        core_tx[j] = share_of(16 * (1 - core) + j).astype(bf16)
        return carry

    lax.fori_loop(0, 16, pack_core, 0)
    to_core = remote(core_tx, core_rx, core_send.at[0], core_recv.at[0], (row, other))
    to_core_s = remote(s_ref, score_rx, core_send.at[1], core_recv.at[1], (row, other))
    to_core.start()

    tap_sums(prest_ref, d_rest_ref, 128, tap_ref, 12)
    to_core.wait()

    def row_copy(j):
        return remote(
            row_tx.at[j],
            row_rx.at[row],
            row_send.at[0, j],
            row_recv.at[0, row],
            (16 * core + j, col),
        )

    def s_row_copy(j):
        return remote(
            srow_tx.at[j],
            srow_rx.at[row],
            row_send.at[1, j],
            row_recv.at[1, row],
            (16 * core + j, col),
        )

    def col_copy(step):
        return remote(
            col_rx.at[col // 2],
            col_rx.at[col // 2],
            col_send.at[0, step],
            col_recv.at[0, col // 2],
            (row, lax.rem(col + step, 8)),
        )

    def s_col_copy(step):
        return remote(
            scol_rx.at[col // 2],
            scol_rx.at[col // 2],
            col_send.at[1, step],
            col_recv.at[1, col // 2],
            (row, lax.rem(col + step, 8)),
        )

    def gather_copy(step):
        peer = 16 * half + lax.rem(place + step, 16)
        return remote(
            gat_tx, gat_rx.at[place], gat_send.at[step], gat_recv.at[place], (peer, col)
        )

    def over_rows(act):
        def step(k, carry):
            j = lax.rem(place + k, 16)

            @pl.when(16 * core + j != row)
            def _():
                act(j)

            return carry

        lax.fori_loop(0, 16, step, 0)

    def over(first, last, act):
        def step(k, carry):
            act(k)
            return carry

        lax.fori_loop(first, last, step, 0)

    def pack_row(j, carry):
        row_tx[j] = (share_of(16 * core + j) + core_rx[j].astype(f32)).astype(bf16)
        return carry

    lax.fori_loop(0, 16, pack_row, 0)
    over_rows(lambda j: row_copy(j).start())

    tap_sums(pmain_ref, d_main_ref, 0, tap_ref, 24)
    taps = jnp.sum(tap_ref[...], axis=1)
    s_ref[0:49, 0:128] = taps[:, 0:128]
    s_ref[0:49, 128:192] = taps[:, 128:192] + taps[:, 192:256]
    s_ref[49:54, 0:channels] = jnp.sum(sums_ref[...], axis=1)
    s_ref[52:53, 0:channels] = s_ref[52:53, 0:channels] * layer_scale_ref[...]
    bias_sum = jnp.sum(bias_sum_ref[...], axis=0, keepdims=True)
    for k in range(4):
        s_ref[54 + k : 55 + k, 0:channels] = bias_sum[:, channels * k : channels * (k + 1)]
    to_core_s.start()

    halo_wait(d_block_ref, d_halo, d_halo_sems, row, col)
    widen_all(d_block_ref, d_halo, True)
    split_rows(main_ref, pmain_ref)
    split_rows(rest_ref, prest_ref)
    part_tiles(prest_ref, ptaps_ref, 128, conv_ref, put_rest, (0, 6))

    to_core_s.wait()
    for j in range(16):
        up, across = 8 * (j // 2), 128 * (j % 2)
        srow_tx[j] = (
            s_ref[up : up + 8, across : across + 128]
            + score_rx[up : up + 8, across : across + 128]
        )
    over_rows(lambda j: s_row_copy(j).start())

    @pl.when(owner)
    def _():
        row_rx[row] = row_tx[place]

        def wait_row(step):
            peer = lax.rem(row + step, 32)
            pltpu.make_async_copy(row_tx.at[0], row_rx.at[peer], row_recv.at[0, peer]).wait()

        over(1, 32, wait_row)

        def add_row(i, carry):
            return carry + row_rx[i].astype(f32)

        total = lax.fori_loop(0, 32, add_row, jnp.zeros((72, 128), f32))
        col_rx[col // 2] = total.astype(bf16)
        over(1, 8, lambda step: col_copy(step).start())

    part_tiles(pmain_ref, ptaps_ref, 0, conv_ref, put_main, (0, 12))

    @pl.when(owner)
    def _():
        srow_rx[row] = srow_tx[place]

        def wait_row(step):
            peer = lax.rem(row + step, 32)
            pltpu.make_async_copy(srow_tx.at[0], srow_rx.at[peer], row_recv.at[1, peer]).wait()

        over(1, 32, wait_row)

        def add_row(i, carry):
            return carry + srow_rx[i]

        scol_rx[col // 2] = lax.fori_loop(0, 32, add_row, jnp.zeros((8, 128), f32))
        over(1, 8, lambda step: s_col_copy(step).start())

    part_tiles(pmain_ref, ptaps_ref, 0, conv_ref, put_main, (12, 18))

    def wait_col(y):
        @pl.when(2 * y + half != col)
        def _():
            pltpu.make_async_copy(scol_rx.at[y], scol_rx.at[y], col_recv.at[1, y]).wait()

    over(0, 4, wait_col)
    gat_tx[...] = ((scol_rx[0] + scol_rx[1]) + (scol_rx[2] + scol_rx[3])) * factor
    over(1, 16, lambda step: gather_copy(step).start())

    part_tiles(pmain_ref, ptaps_ref, 0, conv_ref, put_main, (18, 24))
    part_tiles(prest_ref, ptaps_ref, 128, conv_ref, put_rest, (6, 12))

    def finish(i, carry):
        grad_image_ref[i] = (cot_ref[i].astype(f32) + conv_ref[i]).astype(bf16)
        return carry

    lax.fori_loop(0, n_rows, finish, 0)

    def wait_share(y):
        @pl.when(2 * y + half != col)
        def _():
            pltpu.make_async_copy(col_rx.at[y], col_rx.at[y], col_recv.at[0, y]).wait()

    over(0, 4, wait_share)
    share = jnp.zeros((72, 128), f32)
    for y in range(4):
        share = share + col_rx[y].astype(f32)
    share = share * factor
    share = jnp.concatenate([share[0:24], share[24:48], share[48:72]], axis=1)
    g_in_out_ref[...] = share[:, 0:channels]
    g_out_out_ref[...] = share[:, channels : 2 * channels]

    gat_rx[place] = gat_tx[...]

    def wait_gather(step):
        peer = lax.rem(place + step, 16)
        pltpu.make_async_copy(gat_tx, gat_rx.at[peer], gat_recv.at[peer]).wait()

    over(1, 16, wait_gather)
    for j in range(16):
        up, across = 8 * (j // 2), 128 * (j % 2)
        score_rx[up : up + 8, across : across + 128] = gat_rx[j]
    for a in range(7):
        g_kernel_ref[a] = score_rx[7 * a : 7 * a + 7, 0:channels]
    g_rows_ref[...] = score_rx[48:56, 0:channels]
    picked = jnp.zeros((1, 256), f32)
    for k in range(4):
        picked = picked + jnp.where(row // 8 == k, score_rx[54 + k : 55 + k, :], 0.0)
    picked = pltpu.roll(
        jnp.broadcast_to(picked, (8, 256)), lax.rem(256 - SHARE * lax.rem(row, 8), 256), 1
    )
    g_bias_out_ref[...] = picked[0:1, 0:SHARE]

    halo_send(image_ref, halo, halo_sems, row, col, lambda copy: copy.wait_send())
    halo_send(d_block_ref, d_halo, d_halo_sems, row, col, lambda copy: copy.wait_send())
    over_rows(lambda j: row_copy(j).wait_send())
    over_rows(lambda j: s_row_copy(j).wait_send())

    @pl.when(owner)
    def _():
        over(1, 8, lambda step: col_copy(step).wait_send())
        over(1, 8, lambda step: s_col_copy(step).wait_send())

    over(1, 16, lambda step: gather_copy(step).wait_send())


def fused(image, cotangent, conv_kernel, vectors, in_weight, out_weight_t, factor):
    n_rows, n_cols, channels = image.shape
    hidden_units = in_weight.shape[1]
    vmem = pl.BlockSpec(memory_space=pltpu.VMEM)
    dma = pltpu.SemaphoreType.DMA
    f32, bf16 = jnp.float32, jnp.bfloat16
    halo = [
        pltpu.VMEM((3, n_cols, channels), bf16),
        pltpu.VMEM((3, n_cols, channels), bf16),
        pltpu.VMEM((n_rows + 6, 16, channels), bf16),
        pltpu.VMEM((n_rows + 6, 16, channels), bf16),
    ]
    return pl.pallas_call(
        functools.partial(fused_kernel, factor),
        out_shape=(
            jax.ShapeDtypeStruct(image.shape, bf16),
            jax.ShapeDtypeStruct(image.shape, bf16),
            jax.ShapeDtypeStruct((7, 7, channels), f32),
            jax.ShapeDtypeStruct((8, channels), f32),
            jax.ShapeDtypeStruct((SHARE, channels), f32),
            jax.ShapeDtypeStruct((1, SHARE), f32),
            jax.ShapeDtypeStruct((SHARE, channels), f32),
        ),
        in_specs=[vmem, pl.BlockSpec(memory_space=pl.ANY)] + [vmem] * 9,
        out_specs=(vmem,) * 7,
        scratch_shapes=[
            pltpu.VMEM(image.shape, bf16),
            pltpu.VMEM((56, 256), f32),
            pltpu.VMEM((hidden_units, channels), bf16),
            pltpu.VMEM((hidden_units, channels), bf16),
            pltpu.VMEM((n_rows + 6, 200, 128), f32),
            pltpu.VMEM((n_rows + 6, 104, 128), f32),
            pltpu.VMEM((45, 200, 128), f32),
            pltpu.VMEM((45, 104, 128), f32),
            pltpu.VMEM((18, 8, 256), f32),
            pltpu.VMEM((n_rows, n_cols, channels), f32),
            pltpu.VMEM((n_rows, n_cols, 128), f32),
            pltpu.VMEM((n_rows, n_cols // 2, 128), f32),
            pltpu.VMEM((n_rows, n_cols, channels), bf16),
            *halo,
            *halo,
            pltpu.VMEM((5, 8, channels), f32),
            pltpu.VMEM((49, 8, 256), f32),
            pltpu.VMEM((8, hidden_units), f32),
            pltpu.VMEM((channels, hidden_units), f32),
            pltpu.VMEM((channels, hidden_units), f32),
            pltpu.VMEM((hidden_units, 2 * channels), f32),
            pltpu.VMEM((64, 256), f32),
            pltpu.VMEM((16, 72, 128), bf16),
            pltpu.VMEM((16, 72, 128), bf16),
            pltpu.VMEM((64, 256), f32),
            pltpu.VMEM((16, 72, 128), bf16),
            pltpu.VMEM((16, 8, 128), f32),
            pltpu.VMEM((32, 72, 128), bf16),
            pltpu.VMEM((32, 8, 128), f32),
            pltpu.VMEM((4, 72, 128), bf16),
            pltpu.VMEM((4, 8, 128), f32),
            pltpu.VMEM((8, 128), f32),
            pltpu.VMEM((16, 8, 128), f32),
            dma((2, 8)),
            dma((2, 8)),
            dma((2,)),
            dma((2,)),
            dma((2, 16)),
            dma((2, 32)),
            dma((2, 8)),
            dma((2, 4)),
            dma((16,)),
            dma((16,)),
            dma,
        ],
        compiler_params=pltpu.CompilerParams(
            collective_id=0, has_side_effects=True, vmem_limit_bytes=VMEM_LIMIT
        ),
    )(image, cotangent, conv_kernel, *vectors, in_weight, out_weight_t)


def body(
    image,
    conv_kernel,
    conv_bias,
    norm_gain,
    norm_bias,
    in_weight,
    in_bias,
    out_weight,
    out_bias,
    layer_scale,
    cotangent,
):
    n_rows, n_cols, _ = image.shape
    factor = 1.0 / math.sqrt(n_rows * lax.axis_size("rows") * n_cols * lax.axis_size("cols"))
    vectors = (conv_bias, norm_gain, norm_bias, out_bias, layer_scale, in_bias)
    vectors = [vector[None] for vector in vectors]
    output, grad_image, g_kernel, g_rows, g_in, g_bias, g_out = fused(
        image, cotangent, conv_kernel, vectors, in_weight, out_weight.T, factor
    )
    return (
        output,
        grad_image,
        g_kernel,
        g_rows[1],
        g_rows[2],
        g_rows[3],
        g_in.T,
        g_bias[0],
        g_out,
        g_rows[4],
        g_rows[5],
    )


def solution(mesh):
    placed = (
        P("rows", "cols", None),
        P(),
        P(),
        P(),
        P(),
        P(),
        P(),
        P(),
        P(),
        P(),
        P("rows", "cols", None),
    )
    return jax.shard_map(
        body,
        mesh=mesh,
        in_specs=placed,
        out_specs=(
            P("rows", "cols", None),
            P("rows", "cols", None),
            P(),
            P(),
            P(),
            P(),
            P(None, "rows"),
            P("rows"),
            P("rows", None),
            P(),
            P(),
        ),
        check_vma=False,
    )
```
